512 devices in a mesh: dp: 4 (over y), pipe: 16 (over z_hi, x, core), tensor: 8 (over z_lo).
Axes of the slice: x: 4, y: 4, z: 16 (z_hi: 2, z_lo: 8; z = z_hi * 8 + z_lo), core: 2. Of those that a mesh axis runs over, the one named last changes fastest.
Arguments:
- enc_out: bfloat16 [512, 4096], P('dp', 'tensor'), may hold values from -1.25 to 1.25
- mlp_input: bfloat16 [512, 4096], P('dp', 'tensor'), may hold values from -170 to 170
- grad_kv: bfloat16 [512, 2, 16, 2048], P('dp', None, 'pipe', 'tensor'), may hold values from -1.5 to 1.5
- kv_weight: bfloat16 [4096, 2, 16, 2048], P('dp', None, 'pipe', 'tensor'), may hold values from -0.09375 to 0.09375
- gate_weight: bfloat16 [4096, 16384], P('dp', ('pipe', 'tensor')), may hold values from -0.09375 to 0.09375
- up_weight: bfloat16 [4096, 16384], P('dp', ('pipe', 'tensor')), may hold values from -0.09375 to 0.09375
- down_weight: bfloat16 [16384, 4096], P(('pipe', 'tensor'), 'dp'), may hold values from -0.046875 to 0.046875
- norm_gain: bfloat16 [4096], replicated, may hold values from 0.099609375 to 1.8984375
Outputs:
- input_grad: bfloat16 [512, 4096], P('dp')
- kv_grad: bfloat16 [4096, 2, 16, 2048], P('dp', None, 'pipe', 'tensor')
The draws below stay inside these ranges and needn't reach their ends.
All inputs are finite; a program needn't handle non-finite values.
Results may differ from the reference program's by a relative error of at most 0.009.
Values may be sent and summed in bfloat16 or wider, within the bound.
A program may use at most 64 MiB of HBM per device.

```python
import math
import jax
import jax.numpy as jnp
from jax import lax

D = 4096
TOK = 128
FF = 16384
HEAD_COLS = 2048
LAYERS = 16
TOKENS = 512
N_DP = 4


def draw_mlp_input(key, part):
    key_rows, key_cols, key_base = jax.random.split(key, 3)
    row_scales = jnp.exp(jax.random.uniform(key_rows, (TOKENS, 1), jnp.float32, 0.0, jnp.log(10.0)))
    col_scales = jnp.exp(jax.random.uniform(key_cols, (1, D), jnp.float32, 0.0, jnp.log(10.0)))
    base = jax.random.normal(key_base, (TOKENS, D), jnp.float32)
    base = jnp.clip(base, -5.0, 5.0)
    return (base * row_scales * col_scales / 3.0).astype(jnp.bfloat16)


def level_of(key, dims, cuts, least, top_value):
    def one(axis_at, shards_of):
        steps = jax.random.uniform(jax.random.fold_in(jax.random.fold_in(key, 6), axis_at), (shards_of,), jnp.float32, least / len(cuts), top_value / len(cuts))
        return jnp.repeat(jnp.exp(steps), dims[axis_at] // shards_of).reshape((-1,) + (1,) * (len(dims) - axis_at - 1))

    gain = one(*cuts[0])
    for cut in cuts[1:]:
        gain = gain * one(*cut)
    return gain


def normal_values(rng, dims, deviation, most, shards=(), dtype=jnp.bfloat16):
    values = jax.random.normal(rng, dims, jnp.float32) * deviation
    if len(shards) > 0:
        values = level_of(rng, dims, shards, -0.22, 0.18) * values
    return jnp.clip(values, min=-most, max=most).astype(dtype)


def setup_inputs(seed: int = 0) -> dict:
    streams_of = jax.random.split(jax.random.key(seed), 9)
    enc_out = normal_values(streams_of[0], (TOKENS, D), 0.2, 1.25, ((0, 4), (1, 8)))
    mlp_input = draw_mlp_input(jax.random.fold_in(streams_of[8], 71), 0)
    grad_kv = normal_values(streams_of[2], (TOKENS, 2, LAYERS, HEAD_COLS), 0.25, 1.5, ((0, 4), (2, 16), (3, 8)))
    kv_weight = normal_values(streams_of[3], (D, 2, LAYERS, HEAD_COLS), D ** -0.5, 0.09375, ((0, 4), (2, 16), (3, 8)))
    gate_weight = normal_values(streams_of[4], (D, FF), D ** -0.5, 0.09375, ((0, 4), (1, 128)))
    up_weight = normal_values(streams_of[5], (D, FF), D ** -0.5, 0.09375, ((0, 4), (1, 128)))
    down_weight = normal_values(streams_of[6], (FF, D), FF ** -0.5, 0.046875, ((0, 128), (1, 4)))
    norm_gain = jnp.clip(1.0 + 0.18 * jax.random.normal(streams_of[7], (D,), jnp.float32), 0.099609375, 1.8984375).astype(jnp.bfloat16)
    return dict(enc_out=enc_out, mlp_input=mlp_input, grad_kv=grad_kv, kv_weight=kv_weight, gate_weight=gate_weight, up_weight=up_weight, down_weight=down_weight, norm_gain=norm_gain)


def gelu_parts(preact):
    factor = math.sqrt(2.0 / math.pi)
    tangent = jnp.tanh(factor * (preact + 0.044715 * preact * preact * preact))
    gelu_value = 0.5 * preact * (1.0 + tangent)
    gelu_slope = 0.5 * (1.0 + tangent) + 0.5 * preact * (1.0 - tangent * tangent) * factor * (1.0 + 3.0 * 0.044715 * preact * preact)
    return (gelu_value, gelu_slope)

def reference(enc_out, mlp_input, grad_kv, kv_weight, gate_weight, up_weight, down_weight, norm_gain):
    upstream = jnp.zeros((TOKENS, D), jnp.float32)
    layer_grads = []
    for layer_idx in range(LAYERS):
        grad_here = grad_kv[:, :, layer_idx, :].astype(jnp.float32)
        weight_here = kv_weight[:, :, layer_idx, :].astype(jnp.float32)
        upstream = upstream + jnp.einsum('tsc,dsc->td', grad_here, weight_here)
        summed = jnp.zeros((D, 2, HEAD_COLS), jnp.float32)
        for replica in range(N_DP):
            rows_enc = enc_out[replica * TOK:(replica + 1) * TOK].astype(jnp.float32)
            rows_grad = grad_here[replica * TOK:(replica + 1) * TOK]
            replica_term = jnp.einsum('td,tsc->dsc', rows_enc, rows_grad).astype(jnp.bfloat16)
            replica_term = lax.optimization_barrier(replica_term)
            summed = summed + replica_term.astype(jnp.float32)
        layer_grads.append(summed.astype(jnp.bfloat16))
    kv_grad = jnp.stack(layer_grads, axis=2)
    upstream_half = upstream.astype(jnp.bfloat16)
    values_in = mlp_input.astype(jnp.float32)
    row_scale = lax.rsqrt(lax.optimization_barrier(jnp.mean(values_in * values_in, axis=1, keepdims=True)) + 1e-06)
    gain_row = norm_gain.astype(jnp.float32)
    normed = (values_in * row_scale * gain_row).astype(jnp.bfloat16)
    gate_pre = jnp.dot(normed, gate_weight, preferred_element_type=jnp.float32)
    up_pre = jnp.dot(normed, up_weight, preferred_element_type=jnp.float32)
    hidden_grad = jnp.dot(upstream_half, down_weight.T, preferred_element_type=jnp.float32)
    gelu_value, gelu_slope = gelu_parts(gate_pre)
    gate_grad = (hidden_grad * up_pre * gelu_slope).astype(jnp.bfloat16)
    up_grad = (hidden_grad * gelu_value).astype(jnp.bfloat16)
    normed_grad = jnp.dot(gate_grad, gate_weight.T, preferred_element_type=jnp.float32) + jnp.dot(up_grad, up_weight.T, preferred_element_type=jnp.float32)
    scaled_grad = gain_row * normed_grad
    input_grad = upstream + row_scale * scaled_grad - values_in * (row_scale * row_scale * row_scale) * lax.optimization_barrier(jnp.mean(values_in * scaled_grad, axis=1, keepdims=True))
    return (input_grad.astype(jnp.bfloat16), kv_grad)
```

```python
import math

import jax
import jax.numpy as jnp
from jax import lax
from jax.experimental import pallas as pl
from jax.experimental.pallas import tpu as pltpu
from jax.sharding import PartitionSpec as P

MESH = pl.DeviceIdType.MESH
F32, BF16 = jnp.float32, jnp.bfloat16
NT = (((1,), (1,)), ((), ()))
TN = (((0,), (0,)), ((), ()))


def gelu_parts(preact):
    factor = math.sqrt(2.0 / math.pi)
    tangent = jnp.tanh(factor * (preact + 0.044715 * preact * preact * preact))
    gelu_value = 0.5 * preact * (1.0 + tangent)
    gelu_slope = 0.5 * (1.0 + tangent) + 0.5 * preact * (1.0 - tangent * tangent) * factor * (
        1.0 + 3.0 * 0.044715 * preact * preact
    )
    return (gelu_value, gelu_slope)


def at(index, size):
    return pl.ds(pl.multiple_of(index * size, size), size)


def kernel(
    enc, mlp, grad, kvw, gate, up, down, gain, out, kvg,
    gall, kvv, usend, uown, crecv, xsend, xrecv, ysend, yb, zrecv, upf, ub,
    gu, db, xb, nb, rsb, eb, ee, act, pre, gg, psend, pown, pcrecv, pxsend, pxrecv, pzsend, pzrecv,
    lsem, gsem, wsem, msem, esem, mxsem, mcsem, rcsem, rxsem, rysem, rzsem, azsem, axsem, acsem,
):
    y, pipe, t = lax.axis_index("dp"), lax.axis_index("pipe"), lax.axis_index("tensor")
    zh, x, c = lax.div(pipe, 8), lax.rem(lax.div(pipe, 2), 4), lax.rem(pipe, 2)
    z = zh * 8 + t
    rows = pl.ds(pl.multiple_of(c * 64 + x * 16, 16), 16)
    xrows = pl.ds(pl.multiple_of(x * 16, 16), 16)

    def y_at(d):
        return lax.rem(y + d, 4)

    def x_at(d):
        return lax.rem(x + d, 4)

    def z_at(d):
        return lax.rem(z + d, 16)

    def y_dev(d):
        return {"dp": y_at(d)}

    def x_dev(d):
        return {"pipe": zh * 8 + x_at(d) * 2 + c}

    def z_dev(d):
        peer = z_at(d)
        return {"pipe": lax.div(peer, 8) * 8 + x * 2 + c, "tensor": lax.rem(peer, 8)}

    core_dev = {"pipe": pipe + 1 - 2 * c}

    def remote(src, dst, sems, index, device):
        return pltpu.make_async_remote_copy(
            src_ref=src,
            dst_ref=dst,
            send_sem=sems.at[(0,) + index],
            recv_sem=sems.at[(1,) + index],
            device_id=device,
            device_id_type=MESH,
        )

    barrier = pltpu.get_barrier_semaphore()

    def greet(device):
        pl.semaphore_signal(barrier, inc=1, device_id=device, device_id_type=MESH)

    @pl.loop(1, 16)
    def _(d):
        greet(z_dev(d))

    @pl.loop(1, 4)
    def _(d):
        greet(y_dev(d))
        greet(x_dev(d))

    greet(core_dev)

    own = [
        pltpu.make_async_copy(grad.at[at(0, 64)], gall.at[0, y], lsem.at[0]),
        pltpu.make_async_copy(grad.at[at(1, 64)], gall.at[1, y], lsem.at[1]),
        pltpu.make_async_copy(kvw, kvv, lsem.at[2]),
        pltpu.make_async_copy(mlp.at[rows], xb.at[rows, at(t, 512)], lsem.at[3]),
        pltpu.make_async_copy(enc.at[rows], eb.at[:, at(t, 512)], lsem.at[4]),
        pltpu.make_async_copy(gate, gu.at[at(y, 1024), pl.ds(0, 128)], lsem.at[5]),
        pltpu.make_async_copy(up, gu.at[at(y, 1024), pl.ds(128, 128)], lsem.at[6]),
        pltpu.make_async_copy(down, db.at[:, at(y, 1024)], lsem.at[7]),
    ]
    for copy in own:
        copy.start()

    pl.semaphore_wait(barrier, 22)

    def grad_copy(d, h, to):
        return remote(grad.at[at(h, 64)], gall.at[h, to], gsem, (d, h), y_dev(d))

    def weight_copy(k, d, block):
        src, dst = (
            (gate, gu.at[at(block, 1024), pl.ds(0, 128)]),
            (up, gu.at[at(block, 1024), pl.ds(128, 128)]),
            (down, db.at[:, at(block, 1024)]),
        )[k]
        return remote(src, dst, wsem, (k, d), y_dev(d))

    def lo_copy(k, d, block):
        src = (mlp, enc)[k].at[rows]
        dst = (xb.at[rows, at(block, 512)], eb.at[:, at(block, 512)])[k]
        return remote(src, dst, msem, (k, d), {"tensor": lax.rem(t + d, 8)})

    def enc_y_copy(d, frm):
        return remote(eb.at[:, at(y_at(d), 1024)], ee.at[frm, rows, :], esem, (d,), y_dev(d))

    def side_x_copy(k, d, block):
        r = pl.ds(pl.multiple_of(c * 64 + block * 16, 16), 16)
        src = (xb.at[rows, :], ee.at[:, rows, :])[k]
        dst = (xb.at[r, :], ee.at[:, r, :])[k]
        return remote(src, dst, mxsem, (k, d), x_dev(d))

    def side_core_copy(k, half):
        ref = (xb.at[at(c, 64), :], ee.at[:, at(c, 64), :])[k]
        dst = (xb.at[at(half, 64), :], ee.at[:, at(half, 64), :])[k]
        return remote(ref, dst, mcsem, (k,), core_dev)

    def gather_z_copy(k, d, block):
        ref = (ub, out)[k]
        return remote(ref.at[rows, at(z, 256)], ref.at[rows, at(block, 256)], azsem, (k, d), z_dev(d))

    def gather_x_copy(k, d, block):
        ref = (ub, out)[k]
        r = pl.ds(pl.multiple_of(c * 64 + block * 16, 16), 16)
        return remote(ref.at[rows, :], ref.at[r, :], axsem, (k, d), x_dev(d))

    def gather_core_copy(k, d, half):
        ref = (ub, out)[k]
        block = lax.rem(x + 4 - d, 4)
        src = pl.ds(pl.multiple_of(c * 64 + block * 16, 16), 16)
        dst = pl.ds(pl.multiple_of(half * 64 + block * 16, 16), 16)
        return remote(ref.at[src, :], ref.at[dst, :], acsem, (k, d), core_dev)

    def farthest_first(k):
        j = lax.div(k + 1, 2)
        return 8 + j * (1 - 2 * lax.rem(k, 2))

    def gather(k, before_rows=None):
        @pl.loop(0, 15)
        def _(i):
            d = farthest_first(i)
            gather_z_copy(k, d, z).start()

        if before_rows is not None:
            before_rows()

        @pl.loop(1, 16)
        def _(d):
            gather_z_copy(k, d, z_at(16 - d)).wait_recv()

        for d in (2, 1, 3):
            gather_x_copy(k, d, x).start()
        gather_core_copy(k, 0, c).start()
        for d in (1, 3, 2):
            gather_x_copy(k, d, x_at(4 - d)).wait_recv()
            gather_core_copy(k, d, c).start()
        for d in (0, 1, 3, 2):
            gather_core_copy(k, d, 1 - c).wait_recv()

    for d in (2, 1, 3):
        grad_copy(d, 1 - c, y).start()
    for d in (2, 1, 3):
        grad_copy(d, c, y).start()

    @pl.loop(1, 8)
    def _(d):
        lo_copy(1, d, t).start()

    @pl.loop(1, 8)
    def _(d):
        lo_copy(0, d, t).start()

    for d in (2, 1, 3):
        weight_copy(0, d, y).start()

    own[0].wait()
    own[1].wait()
    own[2].wait()
    for d in (1, 3, 2):
        grad_copy(d, 1 - c, y_at(4 - d)).wait_recv()
    half = lax.dot_general(
        gall[1 - c].reshape(256, 512), kvv[...], NT, preferred_element_type=F32
    )
    usend[...] = half.astype(BF16).reshape(4, 64, 1024)
    ucore = remote(usend, crecv, rcsem, (0,), core_dev)
    ucore.start()
    for d in (1, 3, 2):
        grad_copy(d, c, y_at(4 - d)).wait_recv()
    uown[...] = lax.dot_general(
        gall[c].reshape(256, 512), kvv[...], NT, preferred_element_type=F32
    ).reshape(4, 64, 1024)
    ucore.wait_recv()
    for r in range(4):
        xsend[r] = (uown[r] + crecv[r].astype(F32)).astype(BF16)

    def ux_copy(d):
        return remote(xsend.at[:, at(x_at(d), 16), :], xrecv.at[d], rxsem, (0, d), x_dev(d))

    for d in (2, 1, 3):
        ux_copy(d).start()

    own[3].wait()
    own[4].wait()

    @pl.loop(1, 8)
    def _(d):
        lo_copy(1, d, lax.rem(t + 8 - d, 8)).wait_recv()

    for d in (2, 1, 3):
        enc_y_copy(d, y).start()
    ee[y, rows, :] = eb[:, at(y, 1024)]

    @pl.loop(1, 8)
    def _(d):
        lo_copy(0, d, lax.rem(t + 8 - d, 8)).wait_recv()

    for d in (1, 3, 2):
        ux_copy(d).wait_recv()
    for r in range(4):
        total = uown[r, xrows, :] + crecv[r, xrows, :].astype(F32)
        for d in range(1, 4):
            total = total + xrecv[d, r].astype(F32)
        ysend[r] = total.astype(BF16)

    def uy_copy(d, block):
        return remote(ysend.at[y_at(d)], yb.at[:, at(block, 1024)], rysem, (d,), y_dev(d))

    for d in (2, 1, 3):
        uy_copy(d, y).start()
    yb[:, at(y, 1024)] = ysend[y]

    for d in (1, 3, 2):
        enc_y_copy(d, y_at(4 - d)).wait_recv()
    for k in (0, 1):
        for d in (2, 1, 3):
            side_x_copy(k, d, x).start()
    for d in (1, 3, 2):
        uy_copy(d, y_at(4 - d)).wait_recv()

    def uz_copy(d):
        return remote(yb.at[:, at(z_at(d), 256)], zrecv.at[d], rzsem, (0, d), z_dev(d))

    @pl.loop(0, 15)
    def _(i):
        uz_copy(farthest_first(i)).start()

    for k in (1, 2):
        for d in (2, 1, 3):
            weight_copy(k, d, y).start()

    for k in (0, 1):
        for d in (1, 3, 2):
            side_x_copy(k, d, x_at(4 - d)).wait_recv()
        side_core_copy(k, c).start()

    @pl.loop(1, 16)
    def _(d):
        uz_copy(d).wait_recv()

    total = yb[:, at(z, 256)].astype(F32)
    for d in range(1, 16):
        total = total + zrecv[d].astype(F32)
    upf[...] = total
    ub[rows, at(z, 256)] = total.astype(BF16)

    def meanwhile():
        side_core_copy(0, 1 - c).wait_recv()

        @pl.loop(0, 8)
        def _(i):
            r = at(i, 16)
            values = xb[r, :].astype(F32)
            scale = lax.rsqrt(jnp.mean(values * values, axis=1, keepdims=True) + 1e-06)
            nb[r, :] = (values * scale * gain[...].astype(F32)).astype(BF16)
            rsb[r, :] = jnp.broadcast_to(scale, (16, 128))

        own[5].wait()
        own[6].wait()
        for k in (0, 1):
            for d in (1, 3, 2):
                weight_copy(k, d, y_at(4 - d)).wait_recv()
        pre[...] = jnp.dot(nb[...], gu[...], preferred_element_type=F32)
        value, slope = gelu_parts(pre[:, 0:128])
        act[:, 0:128] = pre[:, 128:256] * slope
        act[:, 128:256] = value
        side_core_copy(1, 1 - c).wait_recv()

        @pl.loop(0, 4)
        def _(i):
            total = jnp.zeros((256, 512), F32)
            for r in range(4):
                g_r = jnp.concatenate([gall[0, r], gall[1, r]], axis=0)
                term = lax.dot_general(ee[r, :, at(i, 256)], g_r, TN, preferred_element_type=F32)
                total = total + term.astype(BF16).astype(F32)
            kvg[at(i, 256), :] = total.astype(BF16)

        own[7].wait()
        for d in (1, 3, 2):
            weight_copy(2, d, y_at(4 - d)).wait_recv()

    gather(0, meanwhile)

    hidden = lax.dot_general(ub[...], db[...], NT, preferred_element_type=F32)
    grads = (jnp.concatenate([hidden, hidden], axis=1) * act[...]).astype(BF16)
    gg[...] = grads
    act[...] = jnp.broadcast_to(
        jnp.sum(grads.astype(F32) * pre[...], axis=1, keepdims=True), (128, 256)
    )

    def term(half, block):
        return lax.dot_general(
            gg[at(half, 64), :], gu[pl.ds(block * 1024, 1024), :], NT, preferred_element_type=F32
        )

    for block in range(4):
        psend[:, pl.ds(block * 1024, 1024)] = term(1 - c, block).astype(BF16)
    psend[:, 4096:4224] = act[at(1 - c, 64), 0:128].astype(BF16)
    pcore = remote(psend, pcrecv, rcsem, (1,), core_dev)
    pcore.start()
    for block in range(4):
        pown[:, pl.ds(block * 1024, 1024)] = term(c, block)
    pown[:, 4096:4224] = act[at(c, 64), 0:128]
    pcore.wait_recv()
    for i in range(4):
        r = pl.ds(i * 16, 16)
        pxsend[r, :] = (pown[r, :] + pcrecv[r, :].astype(F32)).astype(BF16)

    def px_copy(d):
        return remote(pxsend.at[at(x_at(d), 16), :], pxrecv.at[d], rxsem, (1, d), x_dev(d))

    for d in (2, 1, 3):
        px_copy(d).start()
    for d in (1, 3, 2):
        px_copy(d).wait_recv()

    def px_sum(columns):
        total = pown[xrows, columns] + pcrecv[xrows, columns].astype(F32)
        for d in range(1, 4):
            total = total + pxrecv[d, :, columns].astype(F32)
        return total.astype(BF16)

    stat = px_sum(pl.ds(4096, 128))
    for i in range(16):
        pzsend[i, :, 0:256] = px_sum(pl.ds(i * 256, 256))
        pzsend[i, :, 256:384] = stat

    def pz_copy(d):
        return remote(pzsend.at[z_at(d)], pzrecv.at[d], rzsem, (1, d), z_dev(d))

    @pl.loop(0, 15)
    def _(i):
        pz_copy(farthest_first(i)).start()

    @pl.loop(1, 16)
    def _(d):
        pz_copy(d).wait_recv()

    total = pzsend[z].astype(F32)
    for d in range(1, 16):
        total = total + pzrecv[d].astype(F32)
    scale = rsb[rows, 0:1]
    values = xb[rows, at(z, 256)].astype(F32)
    gain_here = gain[:, at(z, 256)].astype(F32)
    result = (
        upf[...]
        + scale * gain_here * total[:, 0:256]
        - values * (scale * scale) * (total[:, 256:257] * (1.0 / 4096.0))
    )
    out[rows, at(z, 256)] = result.astype(BF16)
    gather(1)

    for d in range(1, 4):
        for h in (0, 1):
            grad_copy(d, h, y).wait_send()
        for k in range(3):
            weight_copy(k, d, y).wait_send()
        enc_y_copy(d, y).wait_send()
        for k in (0, 1):
            side_x_copy(k, d, x).wait_send()
            gather_x_copy(k, d, x).wait_send()
        ux_copy(d).wait_send()
        uy_copy(d, y).wait_send()
        px_copy(d).wait_send()
    for k in (0, 1):
        side_core_copy(k, c).wait_send()
        for d in range(4):
            gather_core_copy(k, d, c).wait_send()
    ucore.wait_send()
    pcore.wait_send()

    @pl.loop(1, 8)
    def _(d):
        lo_copy(0, d, t).wait_send()
        lo_copy(1, d, t).wait_send()

    @pl.loop(1, 16)
    def _(d):
        uz_copy(d).wait_send()
        pz_copy(d).wait_send()
        gather_z_copy(0, d, z).wait_send()
        gather_z_copy(1, d, z).wait_send()


def on_device(
    enc_out, mlp_input, grad_kv, kv_weight, gate_weight, up_weight, down_weight, norm_gain
):
    vmem = pl.BlockSpec(memory_space=pltpu.VMEM)
    anywhere = pl.BlockSpec(memory_space=pl.ANY)
    dma = pltpu.SemaphoreType.DMA
    input_grad, kv_grad = pl.pallas_call(
        kernel,
        out_shape=(
            jax.ShapeDtypeStruct((128, 4096), BF16),
            jax.ShapeDtypeStruct((1024, 512), BF16),
        ),
        in_specs=[anywhere] * 7 + [vmem],
        out_specs=(vmem, vmem),
        scratch_shapes=[
            pltpu.VMEM((2, 4, 64, 512), BF16),
            pltpu.VMEM((1024, 512), BF16),
            pltpu.VMEM((4, 64, 1024), BF16),
            pltpu.VMEM((4, 64, 1024), F32),
            pltpu.VMEM((4, 64, 1024), BF16),
            pltpu.VMEM((4, 64, 1024), BF16),
            pltpu.VMEM((4, 4, 16, 1024), BF16),
            pltpu.VMEM((4, 16, 1024), BF16),
            pltpu.VMEM((16, 4096), BF16),
            pltpu.VMEM((16, 16, 256), BF16),
            pltpu.VMEM((16, 256), F32),
            pltpu.VMEM((128, 4096), BF16),
            pltpu.VMEM((4096, 256), BF16),
            pltpu.VMEM((128, 4096), BF16),
            pltpu.VMEM((128, 4096), BF16),
            pltpu.VMEM((128, 4096), BF16),
            pltpu.VMEM((128, 128), F32),
            pltpu.VMEM((16, 4096), BF16),
            pltpu.VMEM((4, 128, 1024), BF16),
            pltpu.VMEM((128, 256), F32),
            pltpu.VMEM((128, 256), F32),
            pltpu.VMEM((128, 256), BF16),
            pltpu.VMEM((64, 4224), BF16),
            pltpu.VMEM((64, 4224), F32),
            pltpu.VMEM((64, 4224), BF16),
            pltpu.VMEM((64, 4224), BF16),
            pltpu.VMEM((4, 16, 4224), BF16),
            pltpu.VMEM((16, 16, 384), BF16),
            pltpu.VMEM((16, 16, 384), BF16),
            dma((8,)),
            dma((2, 4, 2)),
            dma((2, 3, 4)),
            dma((2, 2, 8)),
            dma((2, 4)),
            dma((2, 2, 4)),
            dma((2, 2)),
            dma((2, 2)),
            dma((2, 2, 4)),
            dma((2, 4)),
            dma((2, 2, 16)),
            dma((2, 2, 16)),
            dma((2, 2, 4)),
            dma((2, 2, 4)),
        ],
        compiler_params=pltpu.CompilerParams(collective_id=0, has_side_effects=True),
    )(
        enc_out,
        mlp_input,
        grad_kv.reshape(128, 512),
        kv_weight.reshape(1024, 512),
        gate_weight,
        up_weight,
        down_weight,
        norm_gain.reshape(1, 4096),
    )
    return (input_grad, kv_grad.reshape(1024, 2, 1, 256))


def solution(mesh):
    placed = (
        P("dp", "tensor"),
        P("dp", "tensor"),
        P("dp", None, "pipe", "tensor"),
        P("dp", None, "pipe", "tensor"),
        P("dp", ("pipe", "tensor")),
        P("dp", ("pipe", "tensor")),
        P(("pipe", "tensor"), "dp"),
        P(),
    )
    return jax.shard_map(
        on_device,
        mesh=mesh,
        in_specs=placed,
        out_specs=(P("dp", None), P("dp", None, "pipe", "tensor")),
        check_vma=False,
    )
```

```python
import math

import jax
import jax.numpy as jnp
from jax import lax
from jax.experimental import pallas as pl
from jax.experimental.pallas import tpu as pltpu
from jax.sharding import PartitionSpec as P

MESH = pl.DeviceIdType.MESH
F32, BF16 = jnp.float32, jnp.bfloat16
NT = (((1,), (1,)), ((), ()))
TN = (((0,), (0,)), ((), ()))


def gelu_parts(preact):
    factor = math.sqrt(2.0 / math.pi)
    tangent = jnp.tanh(factor * (preact + 0.044715 * preact * preact * preact))
    gelu_value = 0.5 * preact * (1.0 + tangent)
    gelu_slope = 0.5 * (1.0 + tangent) + 0.5 * preact * (1.0 - tangent * tangent) * factor * (
        1.0 + 3.0 * 0.044715 * preact * preact
    )
    return (gelu_value, gelu_slope)


def at(index, size):
    return pl.ds(pl.multiple_of(index * size, size), size)


def kernel(
    enc, mlp, grad, kvw, gate, up, down, gain, out, kvg,
    gin, kin, gall, kvv, usend, uown, crecv, xsend, xrecv, ysend, yb, zrecv, upf, ub,
    gu, db, xb, nb, rsb, gf, eb, ee, act, pre, gg, psend, pown, pcrecv, pxsend, pxrecv, pzsend, pzrecv,
    szrecv, sxsend, sxrecv, scsend, screcv, left, right,
    lsem, gsem, wsem, msem, esem, mxsem, mcsem, rcsem, rxsem, rysem, rzsem, azsem, axsem, acsem, szsem, sxsem, scsem,
):
    y, pipe, t = lax.axis_index("dp"), lax.axis_index("pipe"), lax.axis_index("tensor")
    zh, x, c = lax.div(pipe, 8), lax.rem(lax.div(pipe, 2), 4), lax.rem(pipe, 2)
    z = zh * 8 + t
    rows = pl.ds(pl.multiple_of(c * 64 + x * 16, 16), 16)
    xrows = pl.ds(pl.multiple_of(x * 16, 16), 16)

    def y_at(d):
        return lax.rem(y + d, 4)

    def x_at(d):
        return lax.rem(x + d, 4)

    def z_at(d):
        return lax.rem(z + d, 16)

    def y_dev(d):
        return {"dp": y_at(d)}

    def x_dev(d):
        return {"pipe": zh * 8 + x_at(d) * 2 + c}

    def z_dev(d):
        peer = z_at(d)
        return {"pipe": lax.div(peer, 8) * 8 + x * 2 + c, "tensor": lax.rem(peer, 8)}

    core_dev = {"pipe": pipe + 1 - 2 * c}

    def remote(src, dst, sems, index, device):
        return pltpu.make_async_remote_copy(
            src_ref=src,
            dst_ref=dst,
            send_sem=sems.at[(0,) + index],
            recv_sem=sems.at[(1,) + index],
            device_id=device,
            device_id_type=MESH,
        )

    barrier = pltpu.get_barrier_semaphore()

    def greet(device):
        pl.semaphore_signal(barrier, inc=1, device_id=device, device_id_type=MESH)

    for d in (1, 2, 3):
        greet(y_dev(d))
        greet(x_dev(d))
    greet(core_dev)
    greet(z_dev(1))
    greet(z_dev(15))

    own = [
        pltpu.make_async_copy(grad, gin, lsem.at[0]),
        pltpu.make_async_copy(kvw, kin, lsem.at[1]),
        pltpu.make_async_copy(mlp.at[rows], xb.at[rows, at(t, 512)], lsem.at[2]),
        pltpu.make_async_copy(enc.at[rows], eb.at[:, at(t, 512)], lsem.at[3]),
        pltpu.make_async_copy(gate, gu.at[at(y, 1024), pl.ds(0, 128)], lsem.at[4]),
        pltpu.make_async_copy(up, gu.at[at(y, 1024), pl.ds(128, 128)], lsem.at[5]),
        pltpu.make_async_copy(down, db.at[:, at(y, 1024)], lsem.at[6]),
    ]
    for copy in own:
        copy.start()
    own[0].wait()
    for h in range(2):
        for k in range(2):
            gall[h, y, :, pl.ds(k * 256, 256)] = gin[pl.ds(h * 64, 64), k, :]

    pl.semaphore_wait(barrier, 9)

    def grad_copy(d, h, to):
        return remote(gall.at[h, y], gall.at[h, to], gsem, (d, h), y_dev(d))

    def weight_part(k, block, p):
        return (
            gu.at[pl.ds(pl.multiple_of(block * 1024 + p * 512, 512), 512), pl.ds(0, 128)],
            gu.at[pl.ds(pl.multiple_of(block * 1024 + p * 512, 512), 512), pl.ds(128, 128)],
            db.at[:, pl.ds(pl.multiple_of(block * 1024 + p * 512, 512), 512)],
        )[k]

    def near_copy(k, way, p, block):
        half = pl.ds(p * 512, 512)
        src = (gate.at[half, :], up.at[half, :], down.at[:, half])[k]
        return remote(src, weight_part(k, block, p), wsem, (k, way, p), y_dev(1 + 2 * way))

    def far_copy(k, p):
        part = weight_part(k, y_at(3 - 2 * p), p)
        return remote(part, part, wsem, (k, 2, p), y_dev(1 + 2 * p))

    def relay(k):
        for p in (0, 1):
            near_copy(k, p, p, y_at(3 - 2 * p)).wait_recv()
            far_copy(k, p).start()

    def weight_here(k):
        own[4 + k].wait()
        for p in (0, 1):
            near_copy(k, 1 - p, p, y_at(1 + 2 * p)).wait_recv()
            part = weight_part(k, y_at(2), p)
            remote(part, part, wsem, (k, 2, p), y_dev(1 + 2 * p)).wait_recv()

    def lo_copy(k, d, block):
        src = (mlp, enc)[k].at[rows]
        dst = (xb.at[rows, at(block, 512)], eb.at[:, at(block, 512)])[k]
        return remote(src, dst, msem, (k, d), {"tensor": lax.rem(t + d, 8)})

    def enc_y_copy(d, frm):
        return remote(eb.at[:, at(y_at(d), 1024)], ee.at[frm, rows, :], esem, (d,), y_dev(d))

    def side_x_copy(k, d, block):
        r = pl.ds(pl.multiple_of(c * 64 + block * 16, 16), 16)
        src = (xb.at[rows, :], ee.at[:, rows, :])[k]
        dst = (xb.at[r, :], ee.at[:, r, :])[k]
        return remote(src, dst, mxsem, (k, d), x_dev(d))

    def side_core_copy(k, half):
        ref = (xb.at[at(c, 64), :], ee.at[:, at(c, 64), :])[k]
        dst = (xb.at[at(half, 64), :], ee.at[:, at(half, 64), :])[k]
        return remote(ref, dst, mcsem, (k,), core_dev)

    def gather_z_copy(k, d, block):
        ref = (ub, out)[k]
        return remote(ref.at[rows, at(z, 256)], ref.at[rows, at(block, 256)], azsem, (k, d), z_dev(d))

    def gather_x_copy(k, d, block):
        ref = (ub, out)[k]
        r = pl.ds(pl.multiple_of(c * 64 + block * 16, 16), 16)
        return remote(ref.at[rows, :], ref.at[r, :], axsem, (k, d), x_dev(d))

    def gather_core_copy(k, d, half):
        ref = (ub, out)[k]
        block = lax.rem(x + 4 - d, 4)
        src = pl.ds(pl.multiple_of(c * 64 + block * 16, 16), 16)
        dst = pl.ds(pl.multiple_of(half * 64 + block * 16, 16), 16)
        return remote(ref.at[src, :], ref.at[dst, :], acsem, (k, d), core_dev)

    def farthest_first(k):
        j = lax.div(k + 1, 2)
        return 8 + j * (1 - 2 * lax.rem(k, 2))

    def gather(k, under_z=None, under_x=None):
        @pl.loop(0, 15)
        def _(i):
            d = farthest_first(i)
            gather_z_copy(k, d, z).start()

        if under_z is not None:
            under_z()

        @pl.loop(1, 16)
        def _(d):
            gather_z_copy(k, d, z_at(16 - d)).wait_recv()

        for d in (2, 1, 3):
            gather_x_copy(k, d, x).start()
        gather_core_copy(k, 0, c).start()
        if under_x is not None:
            under_x()
        for d in (1, 3, 2):
            gather_x_copy(k, d, x_at(4 - d)).wait_recv()
            gather_core_copy(k, d, c).start()
        for d in (0, 1, 3, 2):
            gather_core_copy(k, d, 1 - c).wait_recv()

    def tell(i):
        pl.semaphore_signal(left.at[i], inc=1, device_id=z_dev(2**i), device_id_type=MESH)
        pl.semaphore_signal(right.at[i], inc=1, device_id=z_dev(16 - 2**i), device_id_type=MESH)

    def heard(i):
        pl.semaphore_wait(left.at[i], 1)
        pl.semaphore_wait(right.at[i], 1)

    tell(0)

    for d in (2, 1, 3):
        grad_copy(d, 1 - c, y).start()
    for d in (2, 1, 3):
        grad_copy(d, c, y).start()

    own[1].wait()

    @pl.loop(0, 8)
    def _(i):
        r = at(i, 128)
        for k in range(2):
            kvv[r, pl.ds(k * 256, 256)] = kin[r, k, :]

    heard(0)
    tell(1)
    for d in (1, 3, 2):
        grad_copy(d, 1 - c, y_at(4 - d)).wait_recv()
    half = lax.dot_general(
        gall[1 - c].reshape(256, 512), kvv[...], NT, preferred_element_type=F32
    )
    usend[...] = half.astype(BF16).reshape(4, 64, 1024)
    ucore = remote(usend, crecv, rcsem, (0,), core_dev)
    ucore.start()
    heard(1)
    tell(2)
    for d in (1, 3, 2):
        grad_copy(d, c, y_at(4 - d)).wait_recv()
    for k, way, p in ((0, 0, 0), (0, 1, 1), (0, 0, 1), (0, 1, 0), (1, 0, 0), (1, 1, 1)):
        near_copy(k, way, p, y).start()
    uown[...] = lax.dot_general(
        gall[c].reshape(256, 512), kvv[...], NT, preferred_element_type=F32
    ).reshape(4, 64, 1024)
    ucore.wait_recv()
    for r in range(4):
        xsend[r] = (uown[r] + crecv[r].astype(F32)).astype(BF16)

    def ux_copy(d):
        return remote(xsend.at[:, at(x_at(d), 16), :], xrecv.at[d], rxsem, (0, d), x_dev(d))

    for d in (2, 1, 3):
        ux_copy(d).start()
    heard(2)

    @pl.loop(1, 8)
    def _(d):
        lo_copy(0, d, t).start()

    @pl.loop(1, 8)
    def _(d):
        lo_copy(1, d, t).start()


    for d in (1, 3, 2):
        ux_copy(d).wait_recv()
    for r in range(4):
        total = uown[r, xrows, :] + crecv[r, xrows, :].astype(F32)
        for d in range(1, 4):
            total = total + xrecv[d, r].astype(F32)
        ysend[r] = total.astype(BF16)

    def uy_copy(d, block):
        return remote(ysend.at[y_at(d)], yb.at[:, at(block, 1024)], rysem, (d,), y_dev(d))

    for d in (2, 1, 3):
        uy_copy(d, y).start()
    yb[:, at(y, 1024)] = ysend[y]
    relay(0)
    relay(1)
    for k, way, p in ((1, 0, 1), (1, 1, 0), (2, 0, 0), (2, 1, 1), (2, 0, 1), (2, 1, 0)):
        near_copy(k, way, p, y).start()

    for d in (1, 3, 2):
        uy_copy(d, y_at(4 - d)).wait_recv()

    def uz_copy(d):
        return remote(yb.at[:, at(z_at(d), 256)], zrecv.at[d], rzsem, (0, d), z_dev(d))

    @pl.loop(0, 15)
    def _(i):
        uz_copy(farthest_first(i)).start()

    own[2].wait()

    @pl.loop(1, 8)
    def _(d):
        lo_copy(0, d, lax.rem(t + 8 - d, 8)).wait_recv()

    for d in (2, 1, 3):
        side_x_copy(0, d, x).start()
    own[3].wait()

    @pl.loop(1, 8)
    def _(d):
        lo_copy(1, d, lax.rem(t + 8 - d, 8)).wait_recv()

    for d in (2, 1, 3):
        enc_y_copy(d, y).start()
    ee[y, rows, :] = eb[:, at(y, 1024)]

    @pl.loop(1, 16)
    def _(d):
        uz_copy(d).wait_recv()

    total = yb[:, at(z, 256)].astype(F32)
    for d in range(1, 16):
        total = total + zrecv[d].astype(F32)
    upf[...] = total
    ub[rows, at(z, 256)] = total.astype(BF16)

    def normalize():
        relay(2)
        for d in (1, 3, 2):
            side_x_copy(0, d, x_at(4 - d)).wait_recv()
        side_core_copy(0, c).start()
        side_core_copy(0, 1 - c).wait_recv()
        gf[...] = gain[...].astype(F32)

        @pl.loop(0, 8)
        def _(i):
            r = at(i, 16)
            values = xb[r, :].astype(F32)
            scale = lax.rsqrt(jnp.mean(values * values, axis=1, keepdims=True) + 1e-06)
            rsb[r, :] = jnp.broadcast_to(scale, (16, 128))

        for j in range(32):
            columns = pl.ds(j * 128, 128)
            values = xb[:, columns].astype(F32) * rsb[...]
            nb[:, columns] = (values * gf[j : j + 1, :]).astype(BF16)

    def hidden_units():
        weight_here(0)
        weight_here(1)
        pre[...] = jnp.dot(nb[...], gu[...], preferred_element_type=F32)
        value, slope = gelu_parts(pre[:, 0:128])
        act[:, 0:128] = pre[:, 128:256] * slope
        act[:, 128:256] = value

    def kv_rows():
        side_core_copy(1, 1 - c).wait_recv()

        @pl.loop(0, 4)
        def _(i):
            total = jnp.zeros((256, 512), F32)
            for r in range(4):
                g_r = jnp.concatenate([gall[0, r], gall[1, r]], axis=0)
                term = lax.dot_general(ee[r, :, at(i, 256)], g_r, TN, preferred_element_type=F32)
                total = total + term.astype(BF16).astype(F32)
            total = total.astype(BF16)
            for k in range(2):
                kvg[at(i, 256), k, :] = total[:, k * 256 : k * 256 + 256]

    gather(0, normalize, hidden_units)

    weight_here(2)
    hidden = lax.dot_general(ub[...], db[...], NT, preferred_element_type=F32)
    grads = (jnp.concatenate([hidden, hidden], axis=1) * act[...]).astype(BF16)
    gg[...] = grads
    def term(half, block):
        return lax.dot_general(
            gg[at(half, 64), :], gu[pl.ds(block * 1024, 1024), :], NT, preferred_element_type=F32
        )

    for block in range(4):
        psend[:, pl.ds(block * 1024, 1024)] = term(1 - c, block).astype(BF16)
    pcore = remote(psend, pcrecv, rcsem, (1,), core_dev)
    pcore.start()
    for block in range(4):
        pown[:, pl.ds(block * 1024, 1024)] = term(c, block)

    product = gg[...].astype(F32) * pre[...]
    high = product.astype(BF16)
    low = (product - high.astype(F32)).astype(BF16)
    ones = jnp.ones((8, 256), BF16)
    szrecv[0] = lax.dot_general(ones, high, NT, preferred_element_type=F32) + lax.dot_general(
        ones, low, NT, preferred_element_type=F32
    )

    def sz_copy(d):
        return remote(szrecv.at[0], szrecv.at[d], szsem, (d,), z_dev(d))

    def sx_copy(d):
        return remote(sxsend, sxrecv.at[d], sxsem, (d,), x_dev(d))

    score = remote(scsend, screcv, scsem, (), core_dev)

    @pl.loop(0, 15)
    def _(i):
        sz_copy(farthest_first(i)).start()

    pcore.wait_recv()
    for i in range(4):
        r = pl.ds(i * 16, 16)
        pxsend[r, :] = (pown[r, :] + pcrecv[r, :].astype(F32)).astype(BF16)

    def px_copy(d):
        return remote(pxsend.at[at(x_at(d), 16), :], pxrecv.at[d], rxsem, (1, d), x_dev(d))

    for d in (2, 1, 3):
        px_copy(d).start()
    @pl.loop(1, 16)
    def _(d):
        sz_copy(d).wait_recv()

    total = szrecv[0]
    for d in range(1, 16):
        total = total + szrecv[d]
    sxsend[...] = total
    for d in (2, 1, 3):
        sx_copy(d).start()
    for d in (1, 3, 2):
        px_copy(d).wait_recv()
    for i in range(4):
        columns = pl.ds(i * 1024, 1024)
        total = pown[xrows, columns] + pcrecv[xrows, columns].astype(F32)
        for d in range(1, 4):
            total = total + pxrecv[d, :, columns].astype(F32)
        pzsend[:, columns] = total.astype(BF16)

    def pz_copy(d):
        return remote(pzsend.at[:, at(z_at(d), 256)], pzrecv.at[d], rzsem, (1, d), z_dev(d))

    @pl.loop(0, 15)
    def _(i):
        pz_copy(farthest_first(i)).start()

    for d in (1, 3, 2):
        enc_y_copy(d, y_at(4 - d)).wait_recv()
    for d in (2, 1, 3):
        side_x_copy(1, d, x).start()
    for d in (1, 3, 2):
        sx_copy(d).wait_recv()
    scsend[...] = sxsend[...] + sxrecv[1] + sxrecv[2] + sxrecv[3]
    score.start()
    score.wait_recv()
    stat_row = scsend[0:1, :] + screcv[0:1, :]
    token = c * 64 + x * 16 + lax.broadcasted_iota(jnp.int32, (16, 128), 0)
    mine = lax.broadcasted_iota(jnp.int32, (16, 128), 1) == token
    stat = jnp.sum(jnp.where(mine, jnp.broadcast_to(stat_row, (16, 128)), 0.0), axis=1, keepdims=True)
    scale = rsb[rows, 0:1]
    values = xb[rows, at(z, 256)].astype(F32)
    gain_here = jnp.concatenate([gf[pl.ds(2 * z, 1), :], gf[pl.ds(2 * z + 1, 1), :]], axis=1)
    base = upf[...] - values * (scale * scale) * (stat * (1.0 / 4096.0))

    @pl.loop(1, 16)
    def _(d):
        pz_copy(d).wait_recv()

    for d in (1, 3, 2):
        side_x_copy(1, d, x_at(4 - d)).wait_recv()
    side_core_copy(1, c).start()
    total = pzsend[:, at(z, 256)].astype(F32)
    for d in range(1, 16):
        total = total + pzrecv[d].astype(F32)
    out[rows, at(z, 256)] = (base + scale * gain_here * total).astype(BF16)
    gather(1, kv_rows)

    for d in range(1, 4):
        for h in (0, 1):
            grad_copy(d, h, y).wait_send()
        enc_y_copy(d, y).wait_send()
        for k in (0, 1):
            side_x_copy(k, d, x).wait_send()
            gather_x_copy(k, d, x).wait_send()
        ux_copy(d).wait_send()
        uy_copy(d, y).wait_send()
        px_copy(d).wait_send()
        sx_copy(d).wait_send()
    for k in (0, 1):
        side_core_copy(k, c).wait_send()
        for d in range(4):
            gather_core_copy(k, d, c).wait_send()
    for k in range(3):
        for p in (0, 1):
            near_copy(k, 0, p, y).wait_send()
            near_copy(k, 1, p, y).wait_send()
            far_copy(k, p).wait_send()
    ucore.wait_send()
    score.wait_send()
    pcore.wait_send()

    @pl.loop(1, 8)
    def _(d):
        lo_copy(0, d, t).wait_send()
        lo_copy(1, d, t).wait_send()

    @pl.loop(1, 16)
    def _(d):
        uz_copy(d).wait_send()
        pz_copy(d).wait_send()
        sz_copy(d).wait_send()
        gather_z_copy(0, d, z).wait_send()
        gather_z_copy(1, d, z).wait_send()


def on_device(
    enc_out, mlp_input, grad_kv, kv_weight, gate_weight, up_weight, down_weight, norm_gain
):
    vmem = pl.BlockSpec(memory_space=pltpu.VMEM)
    anywhere = pl.BlockSpec(memory_space=pl.ANY)
    dma = pltpu.SemaphoreType.DMA
    input_grad, kv_grad = pl.pallas_call(
        kernel,
        out_shape=(
            jax.ShapeDtypeStruct((128, 4096), BF16),
            jax.ShapeDtypeStruct((1024, 2, 256), BF16),
        ),
        in_specs=[anywhere] * 7 + [vmem],
        out_specs=(vmem, vmem),
        scratch_shapes=[
            pltpu.VMEM((128, 2, 256), BF16),
            pltpu.VMEM((1024, 2, 256), BF16),
            pltpu.VMEM((2, 4, 64, 512), BF16),
            pltpu.VMEM((1024, 512), BF16),
            pltpu.VMEM((4, 64, 1024), BF16),
            pltpu.VMEM((4, 64, 1024), F32),
            pltpu.VMEM((4, 64, 1024), BF16),
            pltpu.VMEM((4, 64, 1024), BF16),
            pltpu.VMEM((4, 4, 16, 1024), BF16),
            pltpu.VMEM((4, 16, 1024), BF16),
            pltpu.VMEM((16, 4096), BF16),
            pltpu.VMEM((16, 16, 256), BF16),
            pltpu.VMEM((16, 256), F32),
            pltpu.VMEM((128, 4096), BF16),
            pltpu.VMEM((4096, 256), BF16),
            pltpu.VMEM((128, 4096), BF16),
            pltpu.VMEM((128, 4096), BF16),
            pltpu.VMEM((128, 4096), BF16),
            pltpu.VMEM((128, 128), F32),
            pltpu.VMEM((32, 128), F32),
            pltpu.VMEM((16, 4096), BF16),
            pltpu.VMEM((4, 128, 1024), BF16),
            pltpu.VMEM((128, 256), F32),
            pltpu.VMEM((128, 256), F32),
            pltpu.VMEM((128, 256), BF16),
            pltpu.VMEM((64, 4096), BF16),
            pltpu.VMEM((64, 4096), F32),
            pltpu.VMEM((64, 4096), BF16),
            pltpu.VMEM((64, 4096), BF16),
            pltpu.VMEM((4, 16, 4096), BF16),
            pltpu.VMEM((16, 4096), BF16),
            pltpu.VMEM((16, 16, 256), BF16),
            pltpu.VMEM((16, 8, 128), F32),
            pltpu.VMEM((8, 128), F32),
            pltpu.VMEM((4, 8, 128), F32),
            pltpu.VMEM((8, 128), F32),
            pltpu.VMEM((8, 128), F32),
            pltpu.SemaphoreType.REGULAR((3,)),
            pltpu.SemaphoreType.REGULAR((3,)),
            dma((8,)),
            dma((2, 4, 2)),
            dma((2, 3, 3, 2)),
            dma((2, 2, 8)),
            dma((2, 4)),
            dma((2, 2, 4)),
            dma((2, 2)),
            dma((2, 2)),
            dma((2, 2, 4)),
            dma((2, 4)),
            dma((2, 2, 16)),
            dma((2, 2, 16)),
            dma((2, 2, 4)),
            dma((2, 2, 4)),
            dma((2, 16)),
            dma((2, 4)),
            dma((2,)),
        ],
        compiler_params=pltpu.CompilerParams(collective_id=0, has_side_effects=True),
    )(
        enc_out,
        mlp_input,
        grad_kv.reshape(128, 2, 256),
        kv_weight.reshape(1024, 2, 256),
        gate_weight,
        up_weight,
        down_weight,
        norm_gain.reshape(32, 128),
    )
    return (input_grad, kv_grad.reshape(1024, 2, 1, 256))


def solution(mesh):
    placed = (
        P("dp", "tensor"),
        P("dp", "tensor"),
        P("dp", None, "pipe", "tensor"),
        P("dp", None, "pipe", "tensor"),
        P("dp", ("pipe", "tensor")),
        P("dp", ("pipe", "tensor")),
        P(("pipe", "tensor"), "dp"),
        P(),
    )
    return jax.shard_map(
        on_device,
        mesh=mesh,
        in_specs=placed,
        out_specs=(P("dp", None), P("dp", None, "pipe", "tensor")),
        check_vma=False,
    )
```

```python
import math

import jax
import jax.numpy as jnp
from jax import lax
from jax.experimental import pallas as pl
from jax.experimental.pallas import tpu as pltpu
from jax.sharding import PartitionSpec as P

MESH = pl.DeviceIdType.MESH
F32, BF16 = jnp.float32, jnp.bfloat16
NT = (((1,), (1,)), ((), ()))
TN = (((0,), (0,)), ((), ()))


def gelu_parts(preact):
    factor = math.sqrt(2.0 / math.pi)
    tangent = jnp.tanh(factor * (preact + 0.044715 * preact * preact * preact))
    gelu_value = 0.5 * preact * (1.0 + tangent)
    gelu_slope = 0.5 * (1.0 + tangent) + 0.5 * preact * (1.0 - tangent * tangent) * factor * (
        1.0 + 3.0 * 0.044715 * preact * preact
    )
    return (gelu_value, gelu_slope)


def at(index, size):
    return pl.ds(pl.multiple_of(index * size, size), size)


def kernel(
    enc, mlp, grad, kvw, gate, up, down, gain, out, kvg,
    gin, kin, gall, kvv, usend, uown, crecv, xsend, xrecv, ysend, yb, zrecv, upf, ub,
    gu, db, ob, xb, nb, rsb, gf, eb, ee, act, pre, gg, psend, pown, pcrecv, pxsend, pxrecv, pzsend, pzrecv,
    szrecv, sxsend, sxrecv, scsend, screcv, left, right,
    lsem, gsem, wsem, msem, esem, mxsem, mcsem, rcsem, rxsem, rysem, rzsem, azsem, axsem, acsem, szsem, sxsem, scsem, osem,
):
    y, pipe, t = lax.axis_index("dp"), lax.axis_index("pipe"), lax.axis_index("tensor")
    zh, x, c = lax.div(pipe, 8), lax.rem(lax.div(pipe, 2), 4), lax.rem(pipe, 2)
    z = zh * 8 + t
    rows = pl.ds(pl.multiple_of(c * 64 + x * 16, 16), 16)
    xrows = pl.ds(pl.multiple_of(x * 16, 16), 16)

    def y_at(d):
        return lax.rem(y + d, 4)

    def x_at(d):
        return lax.rem(x + d, 4)

    def z_at(d):
        return lax.rem(z + d, 16)

    def y_dev(d):
        return {"dp": y_at(d)}

    def x_dev(d):
        return {"pipe": zh * 8 + x_at(d) * 2 + c}

    def z_dev(d):
        peer = z_at(d)
        return {"pipe": lax.div(peer, 8) * 8 + x * 2 + c, "tensor": lax.rem(peer, 8)}

    core_dev = {"pipe": pipe + 1 - 2 * c}

    def remote(src, dst, sems, index, device):
        return pltpu.make_async_remote_copy(
            src_ref=src,
            dst_ref=dst,
            send_sem=sems.at[(0,) + index],
            recv_sem=sems.at[(1,) + index],
            device_id=device,
            device_id_type=MESH,
        )

    barrier = pltpu.get_barrier_semaphore()

    def greet(device):
        pl.semaphore_signal(barrier, inc=1, device_id=device, device_id_type=MESH)

    for d in (1, 2, 3):
        greet(y_dev(d))
        greet(x_dev(d))
    greet(core_dev)
    greet(z_dev(1))
    greet(z_dev(15))

    own = [
        pltpu.make_async_copy(grad, gin, lsem.at[0]),
        pltpu.make_async_copy(kvw, kin, lsem.at[1]),
        pltpu.make_async_copy(mlp.at[rows], xb.at[rows, at(t, 512)], lsem.at[2]),
        pltpu.make_async_copy(enc.at[rows], eb.at[:, at(t, 512)], lsem.at[3]),
        pltpu.make_async_copy(gate, gu.at[at(y, 1024), pl.ds(0, 128)], lsem.at[4]),
        pltpu.make_async_copy(up, gu.at[at(y, 1024), pl.ds(128, 128)], lsem.at[5]),
        pltpu.make_async_copy(down.at[:, pl.ds(0, 512)], db.at[0, :, at(y, 512)], lsem.at[6]),
        pltpu.make_async_copy(down.at[:, pl.ds(512, 512)], db.at[1, :, at(y, 512)], lsem.at[7]),
    ]
    for copy in own:
        copy.start()
    own[0].wait()
    for h in range(2):
        for k in range(2):
            gall[h, y, :, pl.ds(k * 256, 256)] = gin[pl.ds(h * 64, 64), k, :]

    pl.semaphore_wait(barrier, 9)

    def grad_copy(d, h, to):
        return remote(gall.at[h, y], gall.at[h, to], gsem, (d, h), y_dev(d))

    def weight_part(k, block, p):
        return (
            gu.at[pl.ds(pl.multiple_of(block * 1024 + p * 512, 512), 512), pl.ds(0, 128)],
            gu.at[pl.ds(pl.multiple_of(block * 1024 + p * 512, 512), 512), pl.ds(128, 128)],
            db.at[p, :, at(block, 512)],
        )[k]

    def near_copy(k, way, p, block):
        half = pl.ds(p * 512, 512)
        src = (gate.at[half, :], up.at[half, :], down.at[:, half])[k]
        return remote(src, weight_part(k, block, p), wsem, (k, way, p), y_dev(1 + 2 * way))

    def far_copy(k, p):
        part = weight_part(k, y_at(3 - 2 * p), p)
        return remote(part, part, wsem, (k, 2, p), y_dev(1 + 2 * p))

    def relay(k):
        for p in (0, 1):
            near_copy(k, p, p, y_at(3 - 2 * p)).wait_recv()
            far_copy(k, p).start()

    def weight_here(k):
        own[4 + k].wait()
        for p in (0, 1):
            near_copy(k, 1 - p, p, y_at(1 + 2 * p)).wait_recv()
            part = weight_part(k, y_at(2), p)
            remote(part, part, wsem, (k, 2, p), y_dev(1 + 2 * p)).wait_recv()

    def lo_copy(k, d, block):
        src = (mlp, enc)[k].at[rows]
        dst = (xb.at[rows, at(block, 512)], eb.at[:, at(block, 512)])[k]
        return remote(src, dst, msem, (k, d), {"tensor": lax.rem(t + d, 8)})

    def enc_y_copy(d, frm):
        return remote(eb.at[:, at(y_at(d), 1024)], ee.at[frm, rows, :], esem, (d,), y_dev(d))

    def side_x_copy(k, d, block):
        r = pl.ds(pl.multiple_of(c * 64 + block * 16, 16), 16)
        src = (xb.at[rows, :], ee.at[:, rows, :])[k]
        dst = (xb.at[r, :], ee.at[:, r, :])[k]
        return remote(src, dst, mxsem, (k, d), x_dev(d))

    def side_core_copy(k, half):
        ref = (xb.at[at(c, 64), :], ee.at[:, at(c, 64), :])[k]
        dst = (xb.at[at(half, 64), :], ee.at[:, at(half, 64), :])[k]
        return remote(ref, dst, mcsem, (k,), core_dev)

    def to_core(k, h):
        src, dst = ((usend, crecv), (psend, pcrecv))[k]
        return remote(src.at[h], dst.at[h], rcsem, (k, h), core_dev)

    def to_x(k, h, d):
        if k == 0:
            return remote(
                xsend.at[h, :, at(x_at(d), 16), :], xrecv.at[h, d], rxsem, (k, h, d), x_dev(d)
            )
        return remote(
            pxsend.at[h, at(x_at(d), 16), :], pxrecv.at[h, d], rxsem, (k, h, d), x_dev(d)
        )

    def to_y(h, d, block):
        return remote(
            ysend.at[h, y_at(d)], yb.at[h, :, at(block, 512)], rysem, (h, d), y_dev(d)
        )

    def to_z(k, h, d):
        src, dst = ((yb, zrecv), (pzsend, pzrecv))[k]
        return remote(
            src.at[h, :, at(z_at(d), 128)], dst.at[h, d], rzsem, (k, h, d), z_dev(d)
        )

    def gather_z_copy(k, h, d, block):
        ref = (ub, ob)[k]
        return remote(
            ref.at[h, rows, at(z, 128)], ref.at[h, rows, at(block, 128)], azsem, (k, h, d), z_dev(d)
        )

    def gather_x_copy(k, h, d, block):
        ref = (ub, ob)[k]
        r = pl.ds(pl.multiple_of(c * 64 + block * 16, 16), 16)
        return remote(ref.at[h, rows, :], ref.at[h, r, :], axsem, (k, h, d), x_dev(d))

    def gather_core_copy(k, h, d, half):
        ref = (ub, ob)[k]
        block = lax.rem(x + 4 - d, 4)
        src = pl.ds(pl.multiple_of(c * 64 + block * 16, 16), 16)
        dst = pl.ds(pl.multiple_of(half * 64 + block * 16, 16), 16)
        return remote(ref.at[h, src, :], ref.at[h, dst, :], acsem, (k, h, d), core_dev)

    def out_copy(h, block):
        return pltpu.make_async_copy(
            ob.at[h, :, pl.ds(block * 512, 512)],
            out.at[:, pl.ds(block * 1024 + h * 512, 512)],
            osem.at[h, block],
        )

    def farthest_first(k):
        j = lax.div(k + 1, 2)
        return 8 + j * (1 - 2 * lax.rem(k, 2))

    def send_z(k, h):
        @pl.loop(0, 15)
        def _(i):
            to_z(k, h, farthest_first(i)).start()

    def take_z(k, h):
        @pl.loop(1, 16)
        def _(d):
            to_z(k, h, d).wait_recv()

    def gather_begin(k, h):
        @pl.loop(0, 15)
        def _(i):
            gather_z_copy(k, h, farthest_first(i), z).start()

    def gather_rest(k, under_x=None):
        for h in (0, 1):

            @pl.loop(1, 16)
            def _(d):
                gather_z_copy(k, h, d, z_at(16 - d)).wait_recv()

            for d in (2, 1, 3):
                gather_x_copy(k, h, d, x).start()
            gather_core_copy(k, h, 0, c).start()
        if under_x is not None:
            under_x()
        for h in (0, 1):
            for d in (1, 3, 2):
                gather_x_copy(k, h, d, x_at(4 - d)).wait_recv()
                gather_core_copy(k, h, d, c).start()

    def gather_end(k, h):
        for d in (0, 1, 3, 2):
            gather_core_copy(k, h, d, 1 - c).wait_recv()

    def tell(i):
        pl.semaphore_signal(left.at[i], inc=1, device_id=z_dev(2**i), device_id_type=MESH)
        pl.semaphore_signal(right.at[i], inc=1, device_id=z_dev(16 - 2**i), device_id_type=MESH)

    def heard(i):
        pl.semaphore_wait(left.at[i], 1)
        pl.semaphore_wait(right.at[i], 1)

    tell(0)

    for d in (2, 1, 3):
        grad_copy(d, 1 - c, y).start()
    for d in (2, 1, 3):
        grad_copy(d, c, y).start()

    own[1].wait()

    @pl.loop(0, 8)
    def _(i):
        r = at(i, 128)
        for k in range(2):
            kvv[r, pl.ds(k * 256, 256)] = kin[r, k, :]

    heard(0)
    tell(1)
    for d in (1, 3, 2):
        grad_copy(d, 1 - c, y_at(4 - d)).wait_recv()

    def upstream_part(half, h):
        return lax.dot_general(
            gall[half].reshape(256, 512), kvv[pl.ds(h * 512, 512), :], NT, preferred_element_type=F32
        ).reshape(4, 64, 512)

    for h in (0, 1):
        usend[h] = upstream_part(1 - c, h).astype(BF16)
        to_core(0, h).start()
    heard(1)
    tell(2)
    for d in (1, 3, 2):
        grad_copy(d, c, y_at(4 - d)).wait_recv()
    for way, p in ((0, 0), (1, 1), (0, 1), (1, 0)):
        near_copy(0, way, p, y).start()
    for h in (0, 1):
        uown[h] = upstream_part(c, h)
        to_core(0, h).wait_recv()
        for r in range(4):
            xsend[h, r] = (uown[h, r] + crecv[h, r].astype(F32)).astype(BF16)
        for d in (2, 1, 3):
            to_x(0, h, d).start()
    heard(2)

    @pl.loop(1, 8)
    def _(d):
        lo_copy(0, d, t).start()

    for h in (0, 1):
        for d in (1, 3, 2):
            to_x(0, h, d).wait_recv()
        for r in range(4):
            total = uown[h, r, xrows, :] + crecv[h, r, xrows, :].astype(F32)
            for d in range(1, 4):
                total = total + xrecv[h, d, r].astype(F32)
            ysend[h, r] = total.astype(BF16)
        for d in (2, 1, 3):
            to_y(h, d, y).start()
        yb[h, :, at(y, 512)] = ysend[h, y]
        if h == 0:
            relay(0)
    for h in (0, 1):
        for d in (1, 3, 2):
            to_y(h, d, y_at(4 - d)).wait_recv()
        send_z(0, h)
        if h == 0:
            for way, p in ((0, 0), (1, 1), (0, 1), (1, 0)):
                near_copy(1, way, p, y).start()
    for way, p in ((0, 0), (1, 1), (0, 1), (1, 0)):
        near_copy(2, way, p, y).start()
    own[2].wait()

    @pl.loop(1, 8)
    def _(d):
        lo_copy(0, d, lax.rem(t + 8 - d, 8)).wait_recv()

    for d in (2, 1, 3):
        side_x_copy(0, d, x).start()
    relay(1)
    for h in (0, 1):
        take_z(0, h)
        total = yb[h, :, at(z, 128)].astype(F32)
        for d in range(1, 16):
            total = total + zrecv[h, d].astype(F32)
        upf[h] = total
        ub[h, rows, at(z, 128)] = total.astype(BF16)
        gather_begin(0, h)

    def normalize():
        relay(2)
        for d in (1, 3, 2):
            side_x_copy(0, d, x_at(4 - d)).wait_recv()
        side_core_copy(0, c).start()
        side_core_copy(0, 1 - c).wait_recv()
        gf[...] = gain[...].astype(F32)

        @pl.loop(0, 8)
        def _(i):
            r = at(i, 16)
            values = xb[r, :].astype(F32)
            scale = lax.rsqrt(jnp.mean(values * values, axis=1, keepdims=True) + 1e-06)
            rsb[r, :] = jnp.broadcast_to(scale, (16, 128))

        for j in range(32):
            columns = pl.ds(j * 128, 128)
            values = xb[:, columns].astype(F32) * rsb[...]
            nb[:, columns] = (values * gf[j : j + 1, :]).astype(BF16)

    def hidden_units():
        @pl.loop(1, 8)
        def _(d):
            lo_copy(1, d, t).start()

        weight_here(0)
        weight_here(1)
        pre[...] = jnp.dot(nb[...], gu[...], preferred_element_type=F32)
        value, slope = gelu_parts(pre[:, 0:128])
        act[:, 0:128] = pre[:, 128:256] * slope
        act[:, 128:256] = value

    def kv_rows():
        side_core_copy(1, 1 - c).wait_recv()

        @pl.loop(0, 4)
        def _(i):
            total = jnp.zeros((256, 512), F32)
            for r in range(4):
                g_r = jnp.concatenate([gall[0, r], gall[1, r]], axis=0)
                term = lax.dot_general(ee[r, :, at(i, 256)], g_r, TN, preferred_element_type=F32)
                total = total + term.astype(BF16).astype(F32)
            total = total.astype(BF16)
            for k in range(2):
                kvg[at(i, 256), k, :] = total[:, k * 256 : k * 256 + 256]

    normalize()
    gather_rest(0, hidden_units)
    weight_here(2)
    own[7].wait()

    gather_end(0, 0)
    hidden = lax.dot_general(ub[0], db[0], NT, preferred_element_type=F32)
    gather_end(0, 1)
    hidden = hidden + lax.dot_general(ub[1], db[1], NT, preferred_element_type=F32)
    grads = (jnp.concatenate([hidden, hidden], axis=1) * act[...]).astype(BF16)
    gg[...] = grads
    def term(half, h, block):
        return lax.dot_general(
            gg[at(half, 64), :],
            gu[pl.ds(block * 1024 + h * 512, 512), :],
            NT,
            preferred_element_type=F32,
        )

    for h in (0, 1):
        for block in range(4):
            psend[h, :, pl.ds(block * 512, 512)] = term(1 - c, h, block).astype(BF16)
        to_core(1, h).start()
    for h in (0, 1):
        for block in range(4):
            pown[h, :, pl.ds(block * 512, 512)] = term(c, h, block)
        to_core(1, h).wait_recv()
        for i in range(4):
            r = pl.ds(i * 16, 16)
            pxsend[h, r, :] = (pown[h, r, :] + pcrecv[h, r, :].astype(F32)).astype(BF16)
        for d in (2, 1, 3):
            to_x(1, h, d).start()

    product = gg[...].astype(F32) * pre[...]
    high = product.astype(BF16)
    low = (product - high.astype(F32)).astype(BF16)
    ones = jnp.ones((8, 256), BF16)
    szrecv[0] = lax.dot_general(ones, high, NT, preferred_element_type=F32) + lax.dot_general(
        ones, low, NT, preferred_element_type=F32
    )

    def sz_copy(d):
        return remote(szrecv.at[0], szrecv.at[d], szsem, (d,), z_dev(d))

    def sx_copy(d):
        return remote(sxsend, sxrecv.at[d], sxsem, (d,), x_dev(d))

    score = remote(scsend, screcv, scsem, (), core_dev)

    @pl.loop(0, 15)
    def _(i):
        sz_copy(farthest_first(i)).start()

    own[3].wait()

    @pl.loop(1, 8)
    def _(d):
        lo_copy(1, d, lax.rem(t + 8 - d, 8)).wait_recv()

    for d in (2, 1, 3):
        enc_y_copy(d, y).start()
    ee[y, rows, :] = eb[:, at(y, 1024)]

    for h in (0, 1):
        for d in (1, 3, 2):
            to_x(1, h, d).wait_recv()
        for i in range(2):
            columns = pl.ds(i * 1024, 1024)
            total = pown[h, xrows, columns] + pcrecv[h, xrows, columns].astype(F32)
            for d in range(1, 4):
                total = total + pxrecv[h, d, :, columns].astype(F32)
            pzsend[h, :, columns] = total.astype(BF16)
        send_z(1, h)

    @pl.loop(1, 16)
    def _(d):
        sz_copy(d).wait_recv()

    total = szrecv[0]
    for d in range(1, 16):
        total = total + szrecv[d]
    sxsend[...] = total
    for d in (2, 1, 3):
        sx_copy(d).start()
    for d in (1, 3, 2):
        enc_y_copy(d, y_at(4 - d)).wait_recv()
    for d in (2, 1, 3):
        side_x_copy(1, d, x).start()
    for d in (1, 3, 2):
        sx_copy(d).wait_recv()
    scsend[...] = sxsend[...] + sxrecv[1] + sxrecv[2] + sxrecv[3]
    score.start()
    score.wait_recv()
    stat_row = scsend[0:1, :] + screcv[0:1, :]
    token = c * 64 + x * 16 + lax.broadcasted_iota(jnp.int32, (16, 128), 0)
    mine = lax.broadcasted_iota(jnp.int32, (16, 128), 1) == token
    stat = jnp.sum(jnp.where(mine, jnp.broadcast_to(stat_row, (16, 128)), 0.0), axis=1, keepdims=True)
    scale = rsb[rows, 0:1]
    bases, gains = [], []
    for h in (0, 1):
        column = lax.div(z, 4) * 8 + h * 4 + lax.rem(z, 4)
        values = xb[rows, at(column, 128)].astype(F32)
        bases.append(upf[h] - values * (scale * scale) * (stat * (1.0 / 4096.0)))
        gains.append(scale * gf[pl.ds(column, 1), :])
    for h in (0, 1):
        take_z(1, h)
        total = pzsend[h, :, at(z, 128)].astype(F32)
        for d in range(1, 16):
            total = total + pzrecv[h, d].astype(F32)
        ob[h, rows, at(z, 128)] = (bases[h] + gains[h] * total).astype(BF16)
        gather_begin(1, h)
    for d in (1, 3, 2):
        side_x_copy(1, d, x_at(4 - d)).wait_recv()
    side_core_copy(1, c).start()
    gather_rest(1, kv_rows)
    for h in (0, 1):
        gather_end(1, h)
        for block in range(4):
            out_copy(h, block).start()

    for d in range(1, 4):
        for h in (0, 1):
            grad_copy(d, h, y).wait_send()
        enc_y_copy(d, y).wait_send()
        for k in (0, 1):
            side_x_copy(k, d, x).wait_send()
            for h in (0, 1):
                gather_x_copy(k, h, d, x).wait_send()
                to_x(k, h, d).wait_send()
        to_y(0, d, y).wait_send()
        to_y(1, d, y).wait_send()
        sx_copy(d).wait_send()
    for k in (0, 1):
        side_core_copy(k, c).wait_send()
        for h in (0, 1):
            to_core(k, h).wait_send()
            for d in range(4):
                gather_core_copy(k, h, d, c).wait_send()
    for k in range(3):
        for p in (0, 1):
            near_copy(k, 0, p, y).wait_send()
            near_copy(k, 1, p, y).wait_send()
            far_copy(k, p).wait_send()
    score.wait_send()

    @pl.loop(1, 8)
    def _(d):
        lo_copy(0, d, t).wait_send()
        lo_copy(1, d, t).wait_send()

    @pl.loop(1, 16)
    def _(d):
        sz_copy(d).wait_send()
        for k in (0, 1):
            for h in (0, 1):
                to_z(k, h, d).wait_send()
                gather_z_copy(k, h, d, z).wait_send()

    for h in (0, 1):
        for block in range(4):
            out_copy(h, block).wait()


def on_device(
    enc_out, mlp_input, grad_kv, kv_weight, gate_weight, up_weight, down_weight, norm_gain
):
    vmem = pl.BlockSpec(memory_space=pltpu.VMEM)
    anywhere = pl.BlockSpec(memory_space=pl.ANY)
    dma = pltpu.SemaphoreType.DMA
    input_grad, kv_grad = pl.pallas_call(
        kernel,
        out_shape=(
            jax.ShapeDtypeStruct((128, 4096), BF16),
            jax.ShapeDtypeStruct((1024, 2, 256), BF16),
        ),
        in_specs=[anywhere] * 7 + [vmem],
        out_specs=(anywhere, vmem),
        scratch_shapes=[
            pltpu.VMEM((128, 2, 256), BF16),
            pltpu.VMEM((1024, 2, 256), BF16),
            pltpu.VMEM((2, 4, 64, 512), BF16),
            pltpu.VMEM((1024, 512), BF16),
            pltpu.VMEM((2, 4, 64, 512), BF16),
            pltpu.VMEM((2, 4, 64, 512), F32),
            pltpu.VMEM((2, 4, 64, 512), BF16),
            pltpu.VMEM((2, 4, 64, 512), BF16),
            pltpu.VMEM((2, 4, 4, 16, 512), BF16),
            pltpu.VMEM((2, 4, 16, 512), BF16),
            pltpu.VMEM((2, 16, 2048), BF16),
            pltpu.VMEM((2, 16, 16, 128), BF16),
            pltpu.VMEM((2, 16, 128), F32),
            pltpu.VMEM((2, 128, 2048), BF16),
            pltpu.VMEM((4096, 256), BF16),
            pltpu.VMEM((2, 128, 2048), BF16),
            pltpu.VMEM((2, 128, 2048), BF16),
            pltpu.VMEM((128, 4096), BF16),
            pltpu.VMEM((128, 4096), BF16),
            pltpu.VMEM((128, 128), F32),
            pltpu.VMEM((32, 128), F32),
            pltpu.VMEM((16, 4096), BF16),
            pltpu.VMEM((4, 128, 1024), BF16),
            pltpu.VMEM((128, 256), F32),
            pltpu.VMEM((128, 256), F32),
            pltpu.VMEM((128, 256), BF16),
            pltpu.VMEM((2, 64, 2048), BF16),
            pltpu.VMEM((2, 64, 2048), F32),
            pltpu.VMEM((2, 64, 2048), BF16),
            pltpu.VMEM((2, 64, 2048), BF16),
            pltpu.VMEM((2, 4, 16, 2048), BF16),
            pltpu.VMEM((2, 16, 2048), BF16),
            pltpu.VMEM((2, 16, 16, 128), BF16),
            pltpu.VMEM((16, 8, 128), F32),
            pltpu.VMEM((8, 128), F32),
            pltpu.VMEM((4, 8, 128), F32),
            pltpu.VMEM((8, 128), F32),
            pltpu.VMEM((8, 128), F32),
            pltpu.SemaphoreType.REGULAR((3,)),
            pltpu.SemaphoreType.REGULAR((3,)),
            dma((8,)),
            dma((2, 4, 2)),
            dma((2, 3, 3, 2)),
            dma((2, 2, 8)),
            dma((2, 4)),
            dma((2, 2, 4)),
            dma((2, 2)),
            dma((2, 2, 2)),
            dma((2, 2, 2, 4)),
            dma((2, 2, 4)),
            dma((2, 2, 2, 16)),
            dma((2, 2, 2, 16)),
            dma((2, 2, 2, 4)),
            dma((2, 2, 2, 4)),
            dma((2, 16)),
            dma((2, 4)),
            dma((2,)),
            dma((2, 4)),
        ],
        compiler_params=pltpu.CompilerParams(collective_id=0, has_side_effects=True),
    )(
        enc_out,
        mlp_input,
        grad_kv.reshape(128, 2, 256),
        kv_weight.reshape(1024, 2, 256),
        gate_weight,
        up_weight,
        down_weight,
        norm_gain.reshape(32, 128),
    )
    return (input_grad, kv_grad.reshape(1024, 2, 1, 256))


def solution(mesh):
    placed = (
        P("dp", "tensor"),
        P("dp", "tensor"),
        P("dp", None, "pipe", "tensor"),
        P("dp", None, "pipe", "tensor"),
        P("dp", ("pipe", "tensor")),
        P("dp", ("pipe", "tensor")),
        P(("pipe", "tensor"), "dp"),
        P(),
    )
    return jax.shard_map(
        on_device,
        mesh=mesh,
        in_specs=placed,
        out_specs=(P("dp", None), P("dp", None, "pipe", "tensor")),
        check_vma=False,
    )
```

```python
import math

import jax
import jax.numpy as jnp
from jax import lax
from jax.experimental import pallas as pl
from jax.experimental.pallas import tpu as pltpu
from jax.sharding import PartitionSpec as P

MESH = pl.DeviceIdType.MESH
F32, BF16 = jnp.float32, jnp.bfloat16
NT = (((1,), (1,)), ((), ()))
TN = (((0,), (0,)), ((), ()))


def gelu_parts(preact):
    factor = math.sqrt(2.0 / math.pi)
    tangent = jnp.tanh(factor * (preact + 0.044715 * preact * preact * preact))
    gelu_value = 0.5 * preact * (1.0 + tangent)
    gelu_slope = 0.5 * (1.0 + tangent) + 0.5 * preact * (1.0 - tangent * tangent) * factor * (
        1.0 + 3.0 * 0.044715 * preact * preact
    )
    return (gelu_value, gelu_slope)


def at(index, size):
    return pl.ds(pl.multiple_of(index * size, size), size)


def kernel(
    enc, mlp, grad, kvw, gate, up, down, gain, out, kvg,
    gin, kin, gall, kvv, usend, uown, crecv, xsend, xrecv, ysend, yb, zrecv, upf, ub,
    gu, db, ob, xb, nb, rsb, gb, gf, kvo, eb, ee, act, pre, gg, psend, pown, pcrecv, pxsend, pxrecv, pzsend, pzrecv,
    szrecv, sxsend, sxrecv, scsend, screcv, left, right,
    lsem, gsem, wsem, msem, esem, mxsem, mcsem, rcsem, rxsem, rysem, rzsem, azsem, axsem, acsem, szsem, sxsem, scsem, osem, ksem,
):
    y, pipe, t = lax.axis_index("dp"), lax.axis_index("pipe"), lax.axis_index("tensor")
    zh, x, c = lax.div(pipe, 8), lax.rem(lax.div(pipe, 2), 4), lax.rem(pipe, 2)
    z = zh * 8 + t
    rows = pl.ds(pl.multiple_of(c * 64 + x * 16, 16), 16)
    xrows = pl.ds(pl.multiple_of(x * 16, 16), 16)

    def y_at(d):
        return lax.rem(y + d, 4)

    def x_at(d):
        return lax.rem(x + d, 4)

    def z_at(d):
        return lax.rem(z + d, 16)

    def y_dev(d):
        return {"dp": y_at(d)}

    def x_dev(d):
        return {"pipe": zh * 8 + x_at(d) * 2 + c}

    def z_dev(d):
        peer = z_at(d)
        return {"pipe": lax.div(peer, 8) * 8 + x * 2 + c, "tensor": lax.rem(peer, 8)}

    core_dev = {"pipe": pipe + 1 - 2 * c}

    def remote(src, dst, sems, index, device):
        return pltpu.make_async_remote_copy(
            src_ref=src,
            dst_ref=dst,
            send_sem=sems.at[(0,) + index],
            recv_sem=sems.at[(1,) + index],
            device_id=device,
            device_id_type=MESH,
        )

    barrier = pltpu.get_barrier_semaphore()

    def greet(device):
        pl.semaphore_signal(barrier, inc=1, device_id=device, device_id_type=MESH)

    for d in (1, 2, 3):
        greet(y_dev(d))
        greet(x_dev(d))
    greet(core_dev)
    greet(z_dev(1))
    greet(z_dev(15))

    own = [
        pltpu.make_async_copy(grad, gin, lsem.at[0]),
        pltpu.make_async_copy(kvw, kin, lsem.at[1]),
        pltpu.make_async_copy(mlp.at[rows], xb.at[rows, at(t, 512)], lsem.at[2]),
        pltpu.make_async_copy(enc.at[rows], eb.at[:, at(t, 512)], lsem.at[3]),
        pltpu.make_async_copy(gate, gu.at[at(y, 1024), pl.ds(0, 128)], lsem.at[4]),
        pltpu.make_async_copy(up, gu.at[at(y, 1024), pl.ds(128, 128)], lsem.at[5]),
        pltpu.make_async_copy(down.at[:, pl.ds(0, 512)], db.at[0, :, at(y, 512)], lsem.at[6]),
        pltpu.make_async_copy(down.at[:, pl.ds(512, 512)], db.at[1, :, at(y, 512)], lsem.at[7]),
        pltpu.make_async_copy(gain, gb, lsem.at[8]),
    ]
    for copy in own:
        copy.start()
    own[0].wait()
    for h in range(2):
        for k in range(2):
            gall[h, y, :, pl.ds(k * 256, 256)] = gin[pl.ds(h * 64, 64), k, :]

    pl.semaphore_wait(barrier, 9)

    def grad_copy(d, h, to):
        return remote(gall.at[h, y], gall.at[h, to], gsem, (d, h), y_dev(d))

    def weight_part(k, block, p):
        return (
            gu.at[pl.ds(pl.multiple_of(block * 1024 + p * 512, 512), 512), pl.ds(0, 128)],
            gu.at[pl.ds(pl.multiple_of(block * 1024 + p * 512, 512), 512), pl.ds(128, 128)],
            db.at[p, :, at(block, 512)],
        )[k]

    def near_copy(k, way, p, block):
        half = pl.ds(p * 512, 512)
        src = (gate.at[half, :], up.at[half, :], down.at[:, half])[k]
        return remote(src, weight_part(k, block, p), wsem, (k, way, p), y_dev(1 + 2 * way))

    def far_copy(k, p):
        part = weight_part(k, y_at(3 - 2 * p), p)
        return remote(part, part, wsem, (k, 2, p), y_dev(1 + 2 * p))

    def relay(k):
        for p in (0, 1):
            near_copy(k, p, p, y_at(3 - 2 * p)).wait_recv()
            far_copy(k, p).start()

    def weight_here(k):
        own[4 + k].wait()
        for p in (0, 1):
            near_copy(k, 1 - p, p, y_at(1 + 2 * p)).wait_recv()
            part = weight_part(k, y_at(2), p)
            remote(part, part, wsem, (k, 2, p), y_dev(1 + 2 * p)).wait_recv()

    def lo_copy(k, d, block):
        src = (mlp, enc)[k].at[rows]
        dst = (xb.at[rows, at(block, 512)], eb.at[:, at(block, 512)])[k]
        return remote(src, dst, msem, (k, d), {"tensor": lax.rem(t + d, 8)})

    def enc_y_copy(d, frm):
        return remote(eb.at[:, at(y_at(d), 1024)], ee.at[frm, rows, :], esem, (d,), y_dev(d))

    def side_x_copy(k, d, block):
        r = pl.ds(pl.multiple_of(c * 64 + block * 16, 16), 16)
        src = (xb.at[rows, :], ee.at[:, rows, :])[k]
        dst = (xb.at[r, :], ee.at[:, r, :])[k]
        return remote(src, dst, mxsem, (k, d), x_dev(d))

    def side_core_copy(k, half):
        ref = (xb.at[at(c, 64), :], ee.at[:, at(c, 64), :])[k]
        dst = (xb.at[at(half, 64), :], ee.at[:, at(half, 64), :])[k]
        return remote(ref, dst, mcsem, (k,), core_dev)

    def to_core(k, h):
        src, dst = ((usend, crecv), (psend, pcrecv))[k]
        return remote(src.at[h], dst.at[h], rcsem, (k, h), core_dev)

    def to_x(k, h, d):
        if k == 0:
            return remote(
                xsend.at[h, :, at(x_at(d), 16), :], xrecv.at[h, d], rxsem, (k, h, d), x_dev(d)
            )
        return remote(
            pxsend.at[h, at(x_at(d), 16), :], pxrecv.at[h, d], rxsem, (k, h, d), x_dev(d)
        )

    def to_y(h, d, block):
        return remote(
            ysend.at[h, y_at(d)], yb.at[h, :, at(block, 512)], rysem, (h, d), y_dev(d)
        )

    def to_z(k, h, d):
        src, dst = ((yb, zrecv), (pzsend, pzrecv))[k]
        return remote(
            src.at[h, :, at(z_at(d), 128)], dst.at[h, d], rzsem, (k, h, d), z_dev(d)
        )

    def gather_z_copy(k, h, d, block):
        ref = (ub, ob)[k]
        return remote(
            ref.at[h, rows, at(z, 128)], ref.at[h, rows, at(block, 128)], azsem, (k, h, d), z_dev(d)
        )

    def gather_x_copy(k, h, d, block):
        ref = (ub, ob)[k]
        r = pl.ds(pl.multiple_of(c * 64 + block * 16, 16), 16)
        return remote(ref.at[h, rows, :], ref.at[h, r, :], axsem, (k, h, d), x_dev(d))

    def gather_core_copy(k, h, d, half):
        ref = (ub, ob)[k]
        block = lax.rem(x + 4 - d, 4)
        src = pl.ds(pl.multiple_of(c * 64 + block * 16, 16), 16)
        dst = pl.ds(pl.multiple_of(half * 64 + block * 16, 16), 16)
        return remote(ref.at[h, src, :], ref.at[h, dst, :], acsem, (k, h, d), core_dev)

    def kv_copy(i):
        return pltpu.make_async_copy(kvo.at[at(i, 256)], kvg.at[at(i, 256)], ksem.at[i])

    def out_copy(h, block):
        return pltpu.make_async_copy(
            ob.at[h, :, pl.ds(block * 512, 512)],
            out.at[:, pl.ds(block * 1024 + h * 512, 512)],
            osem.at[h, block],
        )

    def farthest_first(k):
        j = lax.div(k + 1, 2)
        return 8 + j * (1 - 2 * lax.rem(k, 2))

    def send_z(k, h):
        @pl.loop(0, 15)
        def _(i):
            to_z(k, h, farthest_first(i)).start()

    def take_z(k, h):
        @pl.loop(1, 16)
        def _(d):
            to_z(k, h, d).wait_recv()

    def gather_begin(k, h):
        @pl.loop(0, 15)
        def _(i):
            gather_z_copy(k, h, farthest_first(i), z).start()

    def gather_rest(k, under_x=None):
        for h in (0, 1):

            @pl.loop(1, 16)
            def _(d):
                gather_z_copy(k, h, d, z_at(16 - d)).wait_recv()

            for d in (2, 1, 3):
                gather_x_copy(k, h, d, x).start()
            gather_core_copy(k, h, 0, c).start()
        if under_x is not None:
            under_x()
        for h in (0, 1):
            for d in (1, 3, 2):
                gather_x_copy(k, h, d, x_at(4 - d)).wait_recv()
                gather_core_copy(k, h, d, c).start()

    def gather_end(k, h):
        for d in (0, 1, 3, 2):
            gather_core_copy(k, h, d, 1 - c).wait_recv()

    def tell(i):
        pl.semaphore_signal(left.at[i], inc=1, device_id=z_dev(2**i), device_id_type=MESH)
        pl.semaphore_signal(right.at[i], inc=1, device_id=z_dev(16 - 2**i), device_id_type=MESH)

    def heard(i):
        pl.semaphore_wait(left.at[i], 1)
        pl.semaphore_wait(right.at[i], 1)

    tell(0)

    for d in (2, 1, 3):
        grad_copy(d, 1 - c, y).start()
    for d in (2, 1, 3):
        grad_copy(d, c, y).start()

    own[1].wait()

    @pl.loop(0, 8)
    def _(i):
        r = at(i, 128)
        for k in range(2):
            kvv[r, pl.ds(k * 256, 256)] = kin[r, k, :]

    heard(0)
    tell(1)
    for d in (1, 3, 2):
        grad_copy(d, 1 - c, y_at(4 - d)).wait_recv()

    def upstream_part(half, h):
        return lax.dot_general(
            gall[half].reshape(256, 512), kvv[pl.ds(h * 512, 512), :], NT, preferred_element_type=F32
        ).reshape(4, 64, 512)

    for h in (0, 1):
        usend[h] = upstream_part(1 - c, h).astype(BF16)
        to_core(0, h).start()
    heard(1)
    tell(2)
    for d in (1, 3, 2):
        grad_copy(d, c, y_at(4 - d)).wait_recv()
    for way, p in ((0, 0), (1, 1), (0, 1), (1, 0)):
        near_copy(0, way, p, y).start()
    for h in (0, 1):
        uown[h] = upstream_part(c, h)
        to_core(0, h).wait_recv()
        for r in range(4):
            xsend[h, r] = (uown[h, r] + crecv[h, r].astype(F32)).astype(BF16)
        for d in (2, 1, 3):
            to_x(0, h, d).start()
    heard(2)

    @pl.loop(1, 8)
    def _(d):
        lo_copy(0, d, t).start()

    for h in (0, 1):
        for d in (1, 3, 2):
            to_x(0, h, d).wait_recv()
        for r in range(4):
            total = uown[h, r, xrows, :] + crecv[h, r, xrows, :].astype(F32)
            for d in range(1, 4):
                total = total + xrecv[h, d, r].astype(F32)
            ysend[h, r] = total.astype(BF16)
        for d in (2, 1, 3):
            to_y(h, d, y).start()
        yb[h, :, at(y, 512)] = ysend[h, y]
    relay(0)
    for h in (0, 1):
        for d in (1, 3, 2):
            to_y(h, d, y_at(4 - d)).wait_recv()
        send_z(0, h)
        if h == 0:
            for way, p in ((0, 0), (1, 1), (0, 1), (1, 0)):
                near_copy(1, way, p, y).start()
    for way, p in ((0, 0), (1, 1), (0, 1), (1, 0)):
        near_copy(2, way, p, y).start()
    own[2].wait()

    @pl.loop(1, 8)
    def _(d):
        lo_copy(0, d, lax.rem(t + 8 - d, 8)).wait_recv()

    for d in (2, 1, 3):
        side_x_copy(0, d, x).start()
    relay(1)
    for h in (0, 1):
        take_z(0, h)
        total = yb[h, :, at(z, 128)].astype(F32)
        for d in range(1, 16):
            total = total + zrecv[h, d].astype(F32)
        upf[h] = total
        ub[h, rows, at(z, 128)] = total.astype(BF16)
        gather_begin(0, h)

    def hidden_units():
        @pl.loop(1, 8)
        def _(d):
            lo_copy(1, d, t).start()

        side_core_copy(0, 1 - c).wait_recv()
        own[8].wait()
        gf[...] = gb[...].astype(F32)

        @pl.loop(0, 8)
        def _(i):
            r = at(i, 16)
            values = xb[r, :].astype(F32)
            scale = lax.rsqrt(jnp.mean(values * values, axis=1, keepdims=True) + 1e-06)
            rsb[r, :] = jnp.broadcast_to(scale, (16, 128))

        for j in range(32):
            columns = pl.ds(j * 128, 128)
            values = xb[:, columns].astype(F32) * rsb[...]
            nb[:, columns] = (values * gf[j : j + 1, :]).astype(BF16)
        weight_here(0)
        weight_here(1)
        pre[...] = jnp.dot(nb[...], gu[...], preferred_element_type=F32)
        value, slope = gelu_parts(pre[:, 0:128])
        act[:, 0:128] = pre[:, 128:256] * slope
        act[:, 128:256] = value

    def kv_rows():
        side_core_copy(1, 1 - c).wait_recv()

        @pl.loop(0, 4)
        def _(i):
            total = jnp.zeros((256, 512), F32)
            for r in range(4):
                g_r = jnp.concatenate([gall[0, r], gall[1, r]], axis=0)
                term = lax.dot_general(ee[r, :, at(i, 256)], g_r, TN, preferred_element_type=F32)
                total = total + term.astype(BF16).astype(F32)
            total = total.astype(BF16)
            for k in range(2):
                kvo[at(i, 256), k, :] = total[:, k * 256 : k * 256 + 256]
            kv_copy(i).start()

    relay(2)
    for d in (1, 3, 2):
        side_x_copy(0, d, x_at(4 - d)).wait_recv()
    side_core_copy(0, c).start()
    gather_rest(0, hidden_units)
    weight_here(2)
    own[7].wait()

    gather_end(0, 0)
    hidden = lax.dot_general(ub[0], db[0], NT, preferred_element_type=F32)
    gather_end(0, 1)
    hidden = hidden + lax.dot_general(ub[1], db[1], NT, preferred_element_type=F32)
    grads = (jnp.concatenate([hidden, hidden], axis=1) * act[...]).astype(BF16)
    gg[...] = grads
    def term(half, h, block):
        return lax.dot_general(
            gg[at(half, 64), :],
            gu[pl.ds(block * 1024 + h * 512, 512), :],
            NT,
            preferred_element_type=F32,
        )

    for h in (0, 1):
        for block in range(4):
            psend[h, :, pl.ds(block * 512, 512)] = term(1 - c, h, block).astype(BF16)
        to_core(1, h).start()
    for h in (0, 1):
        for block in range(4):
            pown[h, :, pl.ds(block * 512, 512)] = term(c, h, block)
        to_core(1, h).wait_recv()
        for i in range(4):
            r = pl.ds(i * 16, 16)
            pxsend[h, r, :] = (pown[h, r, :] + pcrecv[h, r, :].astype(F32)).astype(BF16)
        for d in (2, 1, 3):
            to_x(1, h, d).start()

    product = gg[...].astype(F32) * pre[...]
    high = product.astype(BF16)
    low = (product - high.astype(F32)).astype(BF16)
    ones = jnp.ones((8, 256), BF16)
    szrecv[0] = lax.dot_general(ones, high, NT, preferred_element_type=F32) + lax.dot_general(
        ones, low, NT, preferred_element_type=F32
    )

    def sz_copy(d):
        return remote(szrecv.at[0], szrecv.at[d], szsem, (d,), z_dev(d))

    def sx_copy(d):
        return remote(sxsend, sxrecv.at[d], sxsem, (d,), x_dev(d))

    score = remote(scsend, screcv, scsem, (), core_dev)

    @pl.loop(0, 15)
    def _(i):
        sz_copy(farthest_first(i)).start()

    own[3].wait()

    @pl.loop(1, 8)
    def _(d):
        lo_copy(1, d, lax.rem(t + 8 - d, 8)).wait_recv()

    for d in (2, 1, 3):
        enc_y_copy(d, y).start()
    ee[y, rows, :] = eb[:, at(y, 1024)]

    for h in (0, 1):
        for d in (1, 3, 2):
            to_x(1, h, d).wait_recv()
        for i in range(2):
            columns = pl.ds(i * 1024, 1024)
            total = pown[h, xrows, columns] + pcrecv[h, xrows, columns].astype(F32)
            for d in range(1, 4):
                total = total + pxrecv[h, d, :, columns].astype(F32)
            pzsend[h, :, columns] = total.astype(BF16)
        send_z(1, h)

    @pl.loop(1, 16)
    def _(d):
        sz_copy(d).wait_recv()

    total = szrecv[0]
    for d in range(1, 16):
        total = total + szrecv[d]
    sxsend[...] = total
    for d in (2, 1, 3):
        sx_copy(d).start()
    for d in (1, 3, 2):
        sx_copy(d).wait_recv()
    scsend[...] = sxsend[...] + sxrecv[1] + sxrecv[2] + sxrecv[3]
    score.start()
    for d in (1, 3, 2):
        enc_y_copy(d, y_at(4 - d)).wait_recv()
    for d in (2, 1, 3):
        side_x_copy(1, d, x).start()
    score.wait_recv()
    stat_row = scsend[0:1, :] + screcv[0:1, :]
    token = c * 64 + x * 16 + lax.broadcasted_iota(jnp.int32, (16, 128), 0)
    mine = lax.broadcasted_iota(jnp.int32, (16, 128), 1) == token
    stat = jnp.sum(jnp.where(mine, jnp.broadcast_to(stat_row, (16, 128)), 0.0), axis=1, keepdims=True)
    scale = rsb[rows, 0:1]
    bases, gains = [], []
    for h in (0, 1):
        column = lax.div(z, 4) * 8 + h * 4 + lax.rem(z, 4)
        values = xb[rows, at(column, 128)].astype(F32)
        bases.append(upf[h] - values * (scale * scale) * (stat * (1.0 / 4096.0)))
        gains.append(scale * gf[pl.ds(column, 1), :])
    for h in (0, 1):
        take_z(1, h)
        total = pzsend[h, :, at(z, 128)].astype(F32)
        for d in range(1, 16):
            total = total + pzrecv[h, d].astype(F32)
        ob[h, rows, at(z, 128)] = (bases[h] + gains[h] * total).astype(BF16)
        gather_begin(1, h)
    for d in (1, 3, 2):
        side_x_copy(1, d, x_at(4 - d)).wait_recv()
    side_core_copy(1, c).start()
    gather_rest(1, kv_rows)
    for h in (0, 1):
        gather_end(1, h)
        for block in range(4):
            out_copy(h, block).start()

    for d in range(1, 4):
        for h in (0, 1):
            grad_copy(d, h, y).wait_send()
        enc_y_copy(d, y).wait_send()
        for k in (0, 1):
            side_x_copy(k, d, x).wait_send()
            for h in (0, 1):
                gather_x_copy(k, h, d, x).wait_send()
                to_x(k, h, d).wait_send()
        to_y(0, d, y).wait_send()
        to_y(1, d, y).wait_send()
        sx_copy(d).wait_send()
    for k in (0, 1):
        side_core_copy(k, c).wait_send()
        for h in (0, 1):
            to_core(k, h).wait_send()
            for d in range(4):
                gather_core_copy(k, h, d, c).wait_send()
    for k in range(3):
        for p in (0, 1):
            near_copy(k, 0, p, y).wait_send()
            near_copy(k, 1, p, y).wait_send()
            far_copy(k, p).wait_send()
    score.wait_send()

    @pl.loop(1, 8)
    def _(d):
        lo_copy(0, d, t).wait_send()
        lo_copy(1, d, t).wait_send()

    @pl.loop(1, 16)
    def _(d):
        sz_copy(d).wait_send()
        for k in (0, 1):
            for h in (0, 1):
                to_z(k, h, d).wait_send()
                gather_z_copy(k, h, d, z).wait_send()

    for h in (0, 1):
        for block in range(4):
            out_copy(h, block).wait()
    for i in range(4):
        kv_copy(i).wait()


def on_device(
    enc_out, mlp_input, grad_kv, kv_weight, gate_weight, up_weight, down_weight, norm_gain
):
    anywhere = pl.BlockSpec(memory_space=pl.ANY)
    dma = pltpu.SemaphoreType.DMA
    input_grad, kv_grad = pl.pallas_call(
        kernel,
        out_shape=(
            jax.ShapeDtypeStruct((128, 4096), BF16),
            jax.ShapeDtypeStruct((1024, 2, 256), BF16),
        ),
        in_specs=[anywhere] * 8,
        out_specs=(anywhere, anywhere),
        scratch_shapes=[
            pltpu.VMEM((128, 2, 256), BF16),
            pltpu.VMEM((1024, 2, 256), BF16),
            pltpu.VMEM((2, 4, 64, 512), BF16),
            pltpu.VMEM((1024, 512), BF16),
            pltpu.VMEM((2, 4, 64, 512), BF16),
            pltpu.VMEM((2, 4, 64, 512), F32),
            pltpu.VMEM((2, 4, 64, 512), BF16),
            pltpu.VMEM((2, 4, 64, 512), BF16),
            pltpu.VMEM((2, 4, 4, 16, 512), BF16),
            pltpu.VMEM((2, 4, 16, 512), BF16),
            pltpu.VMEM((2, 16, 2048), BF16),
            pltpu.VMEM((2, 16, 16, 128), BF16),
            pltpu.VMEM((2, 16, 128), F32),
            pltpu.VMEM((2, 128, 2048), BF16),
            pltpu.VMEM((4096, 256), BF16),
            pltpu.VMEM((2, 128, 2048), BF16),
            pltpu.VMEM((2, 128, 2048), BF16),
            pltpu.VMEM((128, 4096), BF16),
            pltpu.VMEM((128, 4096), BF16),
            pltpu.VMEM((128, 128), F32),
            pltpu.VMEM((32, 128), BF16),
            pltpu.VMEM((32, 128), F32),
            pltpu.VMEM((1024, 2, 256), BF16),
            pltpu.VMEM((16, 4096), BF16),
            pltpu.VMEM((4, 128, 1024), BF16),
            pltpu.VMEM((128, 256), F32),
            pltpu.VMEM((128, 256), F32),
            pltpu.VMEM((128, 256), BF16),
            pltpu.VMEM((2, 64, 2048), BF16),
            pltpu.VMEM((2, 64, 2048), F32),
            pltpu.VMEM((2, 64, 2048), BF16),
            pltpu.VMEM((2, 64, 2048), BF16),
            pltpu.VMEM((2, 4, 16, 2048), BF16),
            pltpu.VMEM((2, 16, 2048), BF16),
            pltpu.VMEM((2, 16, 16, 128), BF16),
            pltpu.VMEM((16, 8, 128), F32),
            pltpu.VMEM((8, 128), F32),
            pltpu.VMEM((4, 8, 128), F32),
            pltpu.VMEM((8, 128), F32),
            pltpu.VMEM((8, 128), F32),
            pltpu.SemaphoreType.REGULAR((3,)),
            pltpu.SemaphoreType.REGULAR((3,)),
            dma((9,)),
            dma((2, 4, 2)),
            dma((2, 3, 3, 2)),
            dma((2, 2, 8)),
            dma((2, 4)),
            dma((2, 2, 4)),
            dma((2, 2)),
            dma((2, 2, 2)),
            dma((2, 2, 2, 4)),
            dma((2, 2, 4)),
            dma((2, 2, 2, 16)),
            dma((2, 2, 2, 16)),
            dma((2, 2, 2, 4)),
            dma((2, 2, 2, 4)),
            dma((2, 16)),
            dma((2, 4)),
            dma((2,)),
            dma((2, 4)),
            dma((4,)),
        ],
        compiler_params=pltpu.CompilerParams(collective_id=0, has_side_effects=True),
    )(
        enc_out,
        mlp_input,
        grad_kv.reshape(128, 2, 256),
        kv_weight.reshape(1024, 2, 256),
        gate_weight,
        up_weight,
        down_weight,
        norm_gain.reshape(32, 128),
    )
    return (input_grad, kv_grad.reshape(1024, 2, 1, 256))


def solution(mesh):
    placed = (
        P("dp", "tensor"),
        P("dp", "tensor"),
        P("dp", None, "pipe", "tensor"),
        P("dp", None, "pipe", "tensor"),
        P("dp", ("pipe", "tensor")),
        P("dp", ("pipe", "tensor")),
        P(("pipe", "tensor"), "dp"),
        P(),
    )
    return jax.shard_map(
        on_device,
        mesh=mesh,
        in_specs=placed,
        out_specs=(P("dp", None), P("dp", None, "pipe", "tensor")),
        check_vma=False,
    )
```

```python
import math

import jax
import jax.numpy as jnp
from jax import lax
from jax.experimental import pallas as pl
from jax.experimental.pallas import tpu as pltpu
from jax.sharding import PartitionSpec as P

MESH = pl.DeviceIdType.MESH
F32, BF16 = jnp.float32, jnp.bfloat16
NT = (((1,), (1,)), ((), ()))
TN = (((0,), (0,)), ((), ()))


def gelu_parts(preact):
    factor = math.sqrt(2.0 / math.pi)
    tangent = jnp.tanh(factor * (preact + 0.044715 * preact * preact * preact))
    gelu_value = 0.5 * preact * (1.0 + tangent)
    gelu_slope = 0.5 * (1.0 + tangent) + 0.5 * preact * (1.0 - tangent * tangent) * factor * (
        1.0 + 3.0 * 0.044715 * preact * preact
    )
    return (gelu_value, gelu_slope)


def at(index, size):
    return pl.ds(pl.multiple_of(index * size, size), size)


def kernel(
    enc, mlp, grad, kvw, gate, up, down, gain, out, kvg,
    gin, kin, gall, kvv, usend, uown, crecv, xsend, xrecv, ysend, yb, zrecv, upf, ub,
    gu, db, ob, xb, nb, rsb, gb, gf, kvo, eb, ee, act, pre, gg, psend, pown, pcrecv, pxsend, pxrecv, pzsend, pzrecv,
    szrecv, sxsend, sxrecv, scsend, screcv, left, right,
    lsem, gsem, wsem, msem, esem, mxsem, mcsem, rcsem, rxsem, rysem, rzsem, azsem, axsem, acsem, szsem, sxsem, scsem, osem, ksem,
):
    y, pipe, t = lax.axis_index("dp"), lax.axis_index("pipe"), lax.axis_index("tensor")
    zh, x, c = lax.div(pipe, 8), lax.rem(lax.div(pipe, 2), 4), lax.rem(pipe, 2)
    z = zh * 8 + t
    rows = pl.ds(pl.multiple_of(c * 64 + x * 16, 16), 16)
    xrows = pl.ds(pl.multiple_of(x * 16, 16), 16)

    def y_at(d):
        return lax.rem(y + d, 4)

    def x_at(d):
        return lax.rem(x + d, 4)

    def z_at(d):
        return lax.rem(z + d, 16)

    def y_dev(d):
        return {"dp": y_at(d)}

    def x_dev(d):
        return {"pipe": zh * 8 + x_at(d) * 2 + c}

    def z_dev(d):
        peer = z_at(d)
        return {"pipe": lax.div(peer, 8) * 8 + x * 2 + c, "tensor": lax.rem(peer, 8)}

    core_dev = {"pipe": pipe + 1 - 2 * c}

    def remote(src, dst, sems, index, device):
        return pltpu.make_async_remote_copy(
            src_ref=src,
            dst_ref=dst,
            send_sem=sems.at[(0,) + index],
            recv_sem=sems.at[(1,) + index],
            device_id=device,
            device_id_type=MESH,
        )

    barrier = pltpu.get_barrier_semaphore()

    def greet(device):
        pl.semaphore_signal(barrier, inc=1, device_id=device, device_id_type=MESH)

    own = [
        pltpu.make_async_copy(grad, gin, lsem.at[0]),
        pltpu.make_async_copy(kvw, kin, lsem.at[1]),
        pltpu.make_async_copy(mlp.at[rows], xb.at[rows, at(t, 512)], lsem.at[2]),
        pltpu.make_async_copy(enc.at[rows], eb.at[:, at(t, 512)], lsem.at[3]),
        pltpu.make_async_copy(gate, gu.at[at(y, 1024), pl.ds(0, 128)], lsem.at[4]),
        pltpu.make_async_copy(up, gu.at[at(y, 1024), pl.ds(128, 128)], lsem.at[5]),
        pltpu.make_async_copy(down.at[:, pl.ds(0, 512)], db.at[0, :, at(y, 512)], lsem.at[6]),
        pltpu.make_async_copy(down.at[:, pl.ds(512, 512)], db.at[1, :, at(y, 512)], lsem.at[7]),
        pltpu.make_async_copy(gain, gb, lsem.at[8]),
    ]
    own[0].start()
    for d in (1, 2, 3):
        greet(y_dev(d))
        greet(x_dev(d))
    greet(core_dev)
    greet(z_dev(1))
    greet(z_dev(15))
    own[1].start()
    own[0].wait()
    for h in range(2):
        for k in range(2):
            gall[h, y, :, pl.ds(k * 256, 256)] = gin[pl.ds(h * 64, 64), k, :]

    pl.semaphore_wait(barrier, 9)

    def grad_copy(d, h, to):
        return remote(gall.at[h, y], gall.at[h, to], gsem, (d, h), y_dev(d))

    def weight_part(k, block, p):
        return (
            gu.at[pl.ds(pl.multiple_of(block * 1024 + p * 512, 512), 512), pl.ds(0, 128)],
            gu.at[pl.ds(pl.multiple_of(block * 1024 + p * 512, 512), 512), pl.ds(128, 128)],
            db.at[p, :, at(block, 512)],
        )[k]

    def near_copy(k, way, p, block):
        half = pl.ds(p * 512, 512)
        src = (gate.at[half, :], up.at[half, :], down.at[:, half])[k]
        return remote(src, weight_part(k, block, p), wsem, (k, way, p), y_dev(1 + 2 * way))

    def far_copy(k, p):
        part = weight_part(k, y_at(3 - 2 * p), p)
        return remote(part, part, wsem, (k, 2, p), y_dev(1 + 2 * p))

    def relay(k):
        for p in (0, 1):
            near_copy(k, p, p, y_at(3 - 2 * p)).wait_recv()
            far_copy(k, p).start()

    def weight_here(k):
        own[4 + k].wait()
        for p in (0, 1):
            near_copy(k, 1 - p, p, y_at(1 + 2 * p)).wait_recv()
            part = weight_part(k, y_at(2), p)
            remote(part, part, wsem, (k, 2, p), y_dev(1 + 2 * p)).wait_recv()

    def lo_copy(k, d, block):
        src = (mlp, enc)[k].at[rows]
        dst = (xb.at[rows, at(block, 512)], eb.at[:, at(block, 512)])[k]
        return remote(src, dst, msem, (k, d), {"tensor": lax.rem(t + d, 8)})

    def enc_y_copy(d, frm):
        return remote(eb.at[:, at(y_at(d), 1024)], ee.at[frm, rows, :], esem, (d,), y_dev(d))

    def side_x_copy(k, d, block):
        r = pl.ds(pl.multiple_of(c * 64 + block * 16, 16), 16)
        src = (xb.at[rows, :], ee.at[:, rows, :])[k]
        dst = (xb.at[r, :], ee.at[:, r, :])[k]
        return remote(src, dst, mxsem, (k, d), x_dev(d))

    def side_core_copy(k, half):
        ref = (xb.at[at(c, 64), :], ee.at[:, at(c, 64), :])[k]
        dst = (xb.at[at(half, 64), :], ee.at[:, at(half, 64), :])[k]
        return remote(ref, dst, mcsem, (k,), core_dev)

    def to_core(k, h):
        src, dst = ((usend, crecv), (psend, pcrecv))[k]
        return remote(src.at[h], dst.at[h], rcsem, (k, h), core_dev)

    def to_x(k, h, d):
        if k == 0:
            return remote(
                xsend.at[h, :, at(x_at(d), 16), :], xrecv.at[h, d], rxsem, (k, h, d), x_dev(d)
            )
        return remote(
            pxsend.at[h, at(x_at(d), 16), :], pxrecv.at[h, d], rxsem, (k, h, d), x_dev(d)
        )

    def to_y(h, d, block):
        return remote(
            ysend.at[h, y_at(d)], yb.at[h, :, at(block, 512)], rysem, (h, d), y_dev(d)
        )

    def to_z(k, h, d):
        src, dst = ((yb, zrecv), (pzsend, pzrecv))[k]
        return remote(
            src.at[h, :, at(z_at(d), 128)], dst.at[h, d], rzsem, (k, h, d), z_dev(d)
        )

    def gather_z_copy(k, h, d, block):
        ref = (ub, ob)[k]
        return remote(
            ref.at[h, rows, at(z, 128)], ref.at[h, rows, at(block, 128)], azsem, (k, h, d), z_dev(d)
        )

    def gather_x_copy(k, h, d, block):
        ref = (ub, ob)[k]
        r = pl.ds(pl.multiple_of(c * 64 + block * 16, 16), 16)
        return remote(ref.at[h, rows, :], ref.at[h, r, :], axsem, (k, h, d), x_dev(d))

    def gather_core_copy(k, h, d, half):
        ref = (ub, ob)[k]
        block = lax.rem(x + 4 - d, 4)
        src = pl.ds(pl.multiple_of(c * 64 + block * 16, 16), 16)
        dst = pl.ds(pl.multiple_of(half * 64 + block * 16, 16), 16)
        return remote(ref.at[h, src, :], ref.at[h, dst, :], acsem, (k, h, d), core_dev)

    def kv_copy(i):
        return pltpu.make_async_copy(kvo.at[at(i, 256)], kvg.at[at(i, 256)], ksem.at[i])

    def out_copy(h, block):
        return pltpu.make_async_copy(
            ob.at[h, :, pl.ds(block * 512, 512)],
            out.at[:, pl.ds(block * 1024 + h * 512, 512)],
            osem.at[h, block],
        )

    def farthest_first(k):
        j = lax.div(k + 1, 2)
        return 8 + j * (1 - 2 * lax.rem(k, 2))

    def send_z(k, h):
        @pl.loop(0, 15)
        def _(i):
            to_z(k, h, farthest_first(i)).start()

    def take_z(k, h):
        @pl.loop(1, 16)
        def _(d):
            to_z(k, h, d).wait_recv()

    def gather_begin(k, h):
        @pl.loop(0, 15)
        def _(i):
            gather_z_copy(k, h, farthest_first(i), z).start()

    def gather_rest(k, under_x=None):
        for h in (0, 1):

            @pl.loop(1, 16)
            def _(d):
                gather_z_copy(k, h, d, z_at(16 - d)).wait_recv()

            for d in (2, 1, 3):
                gather_x_copy(k, h, d, x).start()
            gather_core_copy(k, h, 0, c).start()
        if under_x is not None:
            under_x()
        for h in (0, 1):
            for d in (1, 3, 2):
                gather_x_copy(k, h, d, x_at(4 - d)).wait_recv()
                gather_core_copy(k, h, d, c).start()

    def gather_end(k, h):
        for d in (0, 1, 3, 2):
            gather_core_copy(k, h, d, 1 - c).wait_recv()

    def tell(i):
        pl.semaphore_signal(left.at[i], inc=1, device_id=z_dev(2**i), device_id_type=MESH)
        pl.semaphore_signal(right.at[i], inc=1, device_id=z_dev(16 - 2**i), device_id_type=MESH)

    def heard(i):
        pl.semaphore_wait(left.at[i], 1)
        pl.semaphore_wait(right.at[i], 1)

    tell(0)

    for d in (2, 1, 3):
        grad_copy(d, 1 - c, y).start()
    for d in (2, 1, 3):
        grad_copy(d, c, y).start()

    for copy in own[2:]:
        copy.start()
    own[1].wait()

    @pl.loop(0, 8)
    def _(i):
        r = at(i, 128)
        for k in range(2):
            kvv[r, pl.ds(k * 256, 256)] = kin[r, k, :]

    heard(0)
    tell(1)
    for d in (1, 3, 2):
        grad_copy(d, 1 - c, y_at(4 - d)).wait_recv()

    def upstream_part(half, h):
        return lax.dot_general(
            gall[half].reshape(256, 512), kvv[pl.ds(h * 512, 512), :], NT, preferred_element_type=F32
        ).reshape(4, 64, 512)

    for h in (0, 1):
        usend[h] = upstream_part(1 - c, h).astype(BF16)
        to_core(0, h).start()
    heard(1)
    tell(2)
    for d in (1, 3, 2):
        grad_copy(d, c, y_at(4 - d)).wait_recv()
    for way, p in ((0, 0), (1, 1), (0, 1), (1, 0)):
        near_copy(0, way, p, y).start()
    for h in (0, 1):
        uown[h] = upstream_part(c, h)
        to_core(0, h).wait_recv()
        for r in range(4):
            xsend[h, r] = (uown[h, r] + crecv[h, r].astype(F32)).astype(BF16)
        for d in (2, 1, 3):
            to_x(0, h, d).start()
    heard(2)

    @pl.loop(1, 8)
    def _(d):
        lo_copy(0, d, t).start()

    for h in (0, 1):
        for d in (1, 3, 2):
            to_x(0, h, d).wait_recv()
        for r in range(4):
            total = uown[h, r, xrows, :] + crecv[h, r, xrows, :].astype(F32)
            for d in range(1, 4):
                total = total + xrecv[h, d, r].astype(F32)
            ysend[h, r] = total.astype(BF16)
        for d in (2, 1, 3):
            to_y(h, d, y).start()
        yb[h, :, at(y, 512)] = ysend[h, y]
    relay(0)
    for h in (0, 1):
        for d in (1, 3, 2):
            to_y(h, d, y_at(4 - d)).wait_recv()
        send_z(0, h)
        if h == 0:
            for way, p in ((0, 0), (1, 1), (0, 1), (1, 0)):
                near_copy(1, way, p, y).start()
    for way, p in ((0, 0), (1, 1), (0, 1), (1, 0)):
        near_copy(2, way, p, y).start()
    own[2].wait()

    @pl.loop(1, 8)
    def _(d):
        lo_copy(0, d, lax.rem(t + 8 - d, 8)).wait_recv()

    for d in (2, 1, 3):
        side_x_copy(0, d, x).start()
    relay(1)
    for h in (0, 1):
        take_z(0, h)
        total = yb[h, :, at(z, 128)].astype(F32)
        for d in range(1, 16):
            total = total + zrecv[h, d].astype(F32)
        upf[h] = total
        ub[h, rows, at(z, 128)] = total.astype(BF16)
        gather_begin(0, h)

    def hidden_units():
        @pl.loop(1, 8)
        def _(d):
            lo_copy(1, d, t).start()

        side_core_copy(0, 1 - c).wait_recv()
        own[8].wait()
        gf[...] = gb[...].astype(F32)

        @pl.loop(0, 8)
        def _(i):
            r = at(i, 16)
            values = xb[r, :].astype(F32)
            scale = lax.rsqrt(jnp.mean(values * values, axis=1, keepdims=True) + 1e-06)
            rsb[r, :] = jnp.broadcast_to(scale, (16, 128))

        for j in range(32):
            columns = pl.ds(j * 128, 128)
            values = xb[:, columns].astype(F32) * rsb[...]
            nb[:, columns] = (values * gf[j : j + 1, :]).astype(BF16)
        weight_here(0)
        weight_here(1)
        pre[...] = jnp.dot(nb[...], gu[...], preferred_element_type=F32)
        value, slope = gelu_parts(pre[:, 0:128])
        act[:, 0:128] = pre[:, 128:256] * slope
        act[:, 128:256] = value

    def kv_rows():
        side_core_copy(1, 1 - c).wait_recv()

        @pl.loop(0, 4)
        def _(i):
            total = jnp.zeros((256, 512), F32)
            for r in range(4):
                g_r = jnp.concatenate([gall[0, r], gall[1, r]], axis=0)
                term = lax.dot_general(ee[r, :, at(i, 256)], g_r, TN, preferred_element_type=F32)
                total = total + term.astype(BF16).astype(F32)
            total = total.astype(BF16)
            for k in range(2):
                kvo[at(i, 256), k, :] = total[:, k * 256 : k * 256 + 256]
            kv_copy(i).start()

    relay(2)
    for d in (1, 3, 2):
        side_x_copy(0, d, x_at(4 - d)).wait_recv()
    side_core_copy(0, c).start()
    gather_rest(0, hidden_units)
    weight_here(2)
    own[7].wait()

    gather_end(0, 0)
    hidden = lax.dot_general(ub[0], db[0], NT, preferred_element_type=F32)
    gather_end(0, 1)
    hidden = hidden + lax.dot_general(ub[1], db[1], NT, preferred_element_type=F32)
    grads = (jnp.concatenate([hidden, hidden], axis=1) * act[...]).astype(BF16)
    gg[...] = grads
    def term(half, h, block):
        return lax.dot_general(
            gg[at(half, 64), :],
            gu[pl.ds(block * 1024 + h * 512, 512), :],
            NT,
            preferred_element_type=F32,
        )

    for h in (0, 1):
        for block in range(4):
            psend[h, :, pl.ds(block * 512, 512)] = term(1 - c, h, block).astype(BF16)
        to_core(1, h).start()
    for h in (0, 1):
        for block in range(4):
            pown[h, :, pl.ds(block * 512, 512)] = term(c, h, block)
        to_core(1, h).wait_recv()
        for i in range(4):
            r = pl.ds(i * 16, 16)
            pxsend[h, r, :] = (pown[h, r, :] + pcrecv[h, r, :].astype(F32)).astype(BF16)
        for d in (2, 1, 3):
            to_x(1, h, d).start()

    product = gg[...].astype(F32) * pre[...]
    high = product.astype(BF16)
    low = (product - high.astype(F32)).astype(BF16)
    ones = jnp.ones((8, 256), BF16)
    szrecv[0] = lax.dot_general(ones, high, NT, preferred_element_type=F32) + lax.dot_general(
        ones, low, NT, preferred_element_type=F32
    )

    def sz_copy(d):
        return remote(szrecv.at[0], szrecv.at[d], szsem, (d,), z_dev(d))

    def sx_copy(d):
        return remote(sxsend, sxrecv.at[d], sxsem, (d,), x_dev(d))

    score = remote(scsend, screcv, scsem, (), core_dev)

    @pl.loop(0, 15)
    def _(i):
        sz_copy(farthest_first(i)).start()

    own[3].wait()

    @pl.loop(1, 8)
    def _(d):
        lo_copy(1, d, lax.rem(t + 8 - d, 8)).wait_recv()

    for d in (2, 1, 3):
        enc_y_copy(d, y).start()
    ee[y, rows, :] = eb[:, at(y, 1024)]

    for h in (0, 1):
        for d in (1, 3, 2):
            to_x(1, h, d).wait_recv()
        for i in range(2):
            columns = pl.ds(i * 1024, 1024)
            total = pown[h, xrows, columns] + pcrecv[h, xrows, columns].astype(F32)
            for d in range(1, 4):
                total = total + pxrecv[h, d, :, columns].astype(F32)
            pzsend[h, :, columns] = total.astype(BF16)
        send_z(1, h)

    @pl.loop(1, 16)
    def _(d):
        sz_copy(d).wait_recv()

    total = szrecv[0]
    for d in range(1, 16):
        total = total + szrecv[d]
    sxsend[...] = total
    for d in (2, 1, 3):
        sx_copy(d).start()
    for d in (1, 3, 2):
        sx_copy(d).wait_recv()
    scsend[...] = sxsend[...] + sxrecv[1] + sxrecv[2] + sxrecv[3]
    score.start()
    for d in (1, 3, 2):
        enc_y_copy(d, y_at(4 - d)).wait_recv()
    for d in (2, 1, 3):
        side_x_copy(1, d, x).start()
    score.wait_recv()
    stat_row = scsend[0:1, :] + screcv[0:1, :]
    token = c * 64 + x * 16 + lax.broadcasted_iota(jnp.int32, (16, 128), 0)
    mine = lax.broadcasted_iota(jnp.int32, (16, 128), 1) == token
    stat = jnp.sum(jnp.where(mine, jnp.broadcast_to(stat_row, (16, 128)), 0.0), axis=1, keepdims=True)
    scale = rsb[rows, 0:1]
    bases, gains = [], []
    for h in (0, 1):
        column = lax.div(z, 4) * 8 + h * 4 + lax.rem(z, 4)
        values = xb[rows, at(column, 128)].astype(F32)
        bases.append(upf[h] - values * (scale * scale) * (stat * (1.0 / 4096.0)))
        gains.append(scale * gf[pl.ds(column, 1), :])
    for h in (0, 1):
        take_z(1, h)
        total = pzsend[h, :, at(z, 128)].astype(F32)
        for d in range(1, 16):
            total = total + pzrecv[h, d].astype(F32)
        ob[h, rows, at(z, 128)] = (bases[h] + gains[h] * total).astype(BF16)
        gather_begin(1, h)
    for d in (1, 3, 2):
        side_x_copy(1, d, x_at(4 - d)).wait_recv()
    side_core_copy(1, c).start()
    gather_rest(1, kv_rows)
    for h in (0, 1):
        gather_end(1, h)
        for block in range(4):
            out_copy(h, block).start()

    for d in range(1, 4):
        for h in (0, 1):
            grad_copy(d, h, y).wait_send()
        enc_y_copy(d, y).wait_send()
        for k in (0, 1):
            side_x_copy(k, d, x).wait_send()
            for h in (0, 1):
                gather_x_copy(k, h, d, x).wait_send()
                to_x(k, h, d).wait_send()
        to_y(0, d, y).wait_send()
        to_y(1, d, y).wait_send()
        sx_copy(d).wait_send()
    for k in (0, 1):
        side_core_copy(k, c).wait_send()
        for h in (0, 1):
            to_core(k, h).wait_send()
            for d in range(4):
                gather_core_copy(k, h, d, c).wait_send()
    for k in range(3):
        for p in (0, 1):
            near_copy(k, 0, p, y).wait_send()
            near_copy(k, 1, p, y).wait_send()
            far_copy(k, p).wait_send()
    score.wait_send()

    @pl.loop(1, 8)
    def _(d):
        lo_copy(0, d, t).wait_send()
        lo_copy(1, d, t).wait_send()

    @pl.loop(1, 16)
    def _(d):
        sz_copy(d).wait_send()
        for k in (0, 1):
            for h in (0, 1):
                to_z(k, h, d).wait_send()
                gather_z_copy(k, h, d, z).wait_send()

    for h in (0, 1):
        for block in range(4):
            out_copy(h, block).wait()
    for i in range(4):
        kv_copy(i).wait()


def on_device(
    enc_out, mlp_input, grad_kv, kv_weight, gate_weight, up_weight, down_weight, norm_gain
):
    anywhere = pl.BlockSpec(memory_space=pl.ANY)
    dma = pltpu.SemaphoreType.DMA
    input_grad, kv_grad = pl.pallas_call(
        kernel,
        out_shape=(
            jax.ShapeDtypeStruct((128, 4096), BF16),
            jax.ShapeDtypeStruct((1024, 2, 256), BF16),
        ),
        in_specs=[anywhere] * 8,
        out_specs=(anywhere, anywhere),
        scratch_shapes=[
            pltpu.VMEM((128, 2, 256), BF16),
            pltpu.VMEM((1024, 2, 256), BF16),
            pltpu.VMEM((2, 4, 64, 512), BF16),
            pltpu.VMEM((1024, 512), BF16),
            pltpu.VMEM((2, 4, 64, 512), BF16),
            pltpu.VMEM((2, 4, 64, 512), F32),
            pltpu.VMEM((2, 4, 64, 512), BF16),
            pltpu.VMEM((2, 4, 64, 512), BF16),
            pltpu.VMEM((2, 4, 4, 16, 512), BF16),
            pltpu.VMEM((2, 4, 16, 512), BF16),
            pltpu.VMEM((2, 16, 2048), BF16),
            pltpu.VMEM((2, 16, 16, 128), BF16),
            pltpu.VMEM((2, 16, 128), F32),
            pltpu.VMEM((2, 128, 2048), BF16),
            pltpu.VMEM((4096, 256), BF16),
            pltpu.VMEM((2, 128, 2048), BF16),
            pltpu.VMEM((2, 128, 2048), BF16),
            pltpu.VMEM((128, 4096), BF16),
            pltpu.VMEM((128, 4096), BF16),
            pltpu.VMEM((128, 128), F32),
            pltpu.VMEM((32, 128), BF16),
            pltpu.VMEM((32, 128), F32),
            pltpu.VMEM((1024, 2, 256), BF16),
            pltpu.VMEM((16, 4096), BF16),
            pltpu.VMEM((4, 128, 1024), BF16),
            pltpu.VMEM((128, 256), F32),
            pltpu.VMEM((128, 256), F32),
            pltpu.VMEM((128, 256), BF16),
            pltpu.VMEM((2, 64, 2048), BF16),
            pltpu.VMEM((2, 64, 2048), F32),
            pltpu.VMEM((2, 64, 2048), BF16),
            pltpu.VMEM((2, 64, 2048), BF16),
            pltpu.VMEM((2, 4, 16, 2048), BF16),
            pltpu.VMEM((2, 16, 2048), BF16),
            pltpu.VMEM((2, 16, 16, 128), BF16),
            pltpu.VMEM((16, 8, 128), F32),
            pltpu.VMEM((8, 128), F32),
            pltpu.VMEM((4, 8, 128), F32),
            pltpu.VMEM((8, 128), F32),
            pltpu.VMEM((8, 128), F32),
            pltpu.SemaphoreType.REGULAR((3,)),
            pltpu.SemaphoreType.REGULAR((3,)),
            dma((9,)),
            dma((2, 4, 2)),
            dma((2, 3, 3, 2)),
            dma((2, 2, 8)),
            dma((2, 4)),
            dma((2, 2, 4)),
            dma((2, 2)),
            dma((2, 2, 2)),
            dma((2, 2, 2, 4)),
            dma((2, 2, 4)),
            dma((2, 2, 2, 16)),
            dma((2, 2, 2, 16)),
            dma((2, 2, 2, 4)),
            dma((2, 2, 2, 4)),
            dma((2, 16)),
            dma((2, 4)),
            dma((2,)),
            dma((2, 4)),
            dma((4,)),
        ],
        compiler_params=pltpu.CompilerParams(collective_id=0, has_side_effects=True),
    )(
        enc_out,
        mlp_input,
        grad_kv.reshape(128, 2, 256),
        kv_weight.reshape(1024, 2, 256),
        gate_weight,
        up_weight,
        down_weight,
        norm_gain.reshape(32, 128),
    )
    return (input_grad, kv_grad.reshape(1024, 2, 1, 256))


def solution(mesh):
    placed = (
        P("dp", "tensor"),
        P("dp", "tensor"),
        P("dp", None, "pipe", "tensor"),
        P("dp", None, "pipe", "tensor"),
        P("dp", ("pipe", "tensor")),
        P("dp", ("pipe", "tensor")),
        P(("pipe", "tensor"), "dp"),
        P(),
    )
    return jax.shard_map(
        on_device,
        mesh=mesh,
        in_specs=placed,
        out_specs=(P("dp", None), P("dp", None, "pipe", "tensor")),
        check_vma=False,
    )
```
